32 devices in a mesh: dp: 8 (over z, y), tensor: 4 (over x, core).
Axes of the slice: x: 2, y: 2, z: 4, core: 2. Of those that a mesh axis runs over, the one named last changes fastest.
Arguments:
- layer_input: bfloat16 [16384, 1024], P('dp'), may hold values from -6 to 6
- positions: int32 [16384], P('dp'), may hold values from 0 to 2047, as said below
- block_ids: int32 [16384], P('dp'), may hold values from 0 to 31, as said below
- ln_gain: float32 [1024], replicated, may hold values from 0.5 to 1.5
- ln_bias: float32 [1024], replicated, may hold values from -1 to 1
- w_qkv: bfloat16 [1024, 3072], P(None, 'tensor'), may hold values from -0.1875 to 0.1875
- b_qkv: float32 [3072], P('tensor'), may hold values from -1 to 1
- w_dense: bfloat16 [1024, 1024], P('tensor'), may hold values from -0.75 to 0.75
- b_dense: float32 [1024], replicated, may hold values from -1 to 1
- w_in: bfloat16 [1024, 4096], P(None, 'tensor'), may hold values from -0.1875 to 0.1875
- b_in: float32 [4096], P('tensor'), may hold values from -1 to 1
- w_out: bfloat16 [4096, 1024], P('tensor'), may hold values from -0.09375 to 0.09375
- b_out: float32 [1024], replicated, may hold values from -1 to 1
- cotangent: bfloat16 [16384, 1024], P('dp'), may hold values from -6 to 6
Outputs:
- output: bfloat16 [16384, 1024], P('dp')
- grad_input: float32 [16384, 1024], P('dp')
- grad_ln_gain: float32 [1024], replicated
- grad_ln_bias: float32 [1024], replicated
- grad_w_qkv: float32 [1024, 3072], P(None, 'tensor')
- grad_b_qkv: float32 [3072], P('tensor')
- grad_w_dense: float32 [1024, 1024], P('tensor')
- grad_b_dense: float32 [1024], replicated
- grad_w_in: float32 [1024, 4096], P(None, 'tensor')
- grad_b_in: float32 [4096], P('tensor')
- grad_w_out: float32 [4096, 1024], P('tensor')
- grad_b_out: float32 [1024], replicated
The draws below stay inside these ranges and needn't reach their ends.
Inputs may be any that keep to these rules, and one draw needn't show every extreme that they name: Each sequence of 2048 tokens packs up to four documents: positions rise by one from token to token and return to 0 where a document starts. The first sequence is one document. block_ids = (s + t) // 256 for the t-th token of a sequence, with an offset s of 0 to 6144 for each sequence, 0 for the first and 6144 for the last.
All inputs are finite; a program needn't handle non-finite values.
Results may differ from the reference program's by a relative error of at most 0.008.
Values sent between devices are 32-bit elements; how exact they have to be, the bound alone decides.
A program may use at most 192 MiB of HBM per device.

```python
import jax
import jax.numpy as jnp
from jax import lax

D = 1024
HEADS = 16
HD = 64
FF = 4096
ROT = 16
SEQ = 2048
BLOCK = 256
QBLOCK = 512
TOKENS = 16384


def sequence_starts(key):
    seq_count = TOKENS // SEQ
    starts = jax.random.randint(jax.random.fold_in(key, 11), (seq_count,), 0, 3 * SEQ + 1)
    starts = starts.at[0].set(0)
    return starts.at[seq_count - 1].set(3 * SEQ)


def document_cuts(key):
    seq_count = TOKENS // SEQ
    cuts = jax.random.randint(jax.random.fold_in(key, 23), (seq_count, 3), 1, SEQ)
    return cuts.at[0].set(0)


def draw_positions(key, part):
    cuts = document_cuts(key)
    offsets = jnp.arange(SEQ, dtype=jnp.int32)
    passed = cuts[:, None, :] <= offsets[None, :, None]
    last_cut = jnp.max(jnp.where(passed, cuts[:, None, :], 0), axis=-1)
    return (offsets[None, :] - last_cut).reshape(TOKENS).astype(jnp.int32)


def draw_block_ids(key, part):
    starts = sequence_starts(key)
    offsets = jnp.arange(SEQ, dtype=jnp.int32)
    return ((starts[:, None] + offsets[None, :]) // BLOCK).reshape(TOKENS).astype(jnp.int32)


def block_scale(rng, extent, split, low, top_value):
    def one(axis_at, shards_of):
        draws = jax.random.uniform(jax.random.fold_in(jax.random.fold_in(rng, 6), axis_at), (shards_of,), jnp.float32, low / len(split), top_value / len(split))
        return jnp.repeat(jnp.exp(draws), extent[axis_at] // shards_of).reshape((-1,) + (1,) * (len(extent) - axis_at - 1))

    level = one(*split[0])
    for cut in split[1:]:
        level = level * one(*cut)
    return level


def normal_values(stream_key, shape, scale, bound, cuts=(), held_as=jnp.bfloat16):
    array = scale * jax.random.normal(stream_key, shape, jnp.float32)
    if cuts:
        array = array * block_scale(stream_key, shape, cuts, -0.22, 0.18)
    return jnp.clip(array, -bound, bound).astype(held_as)


def setup_inputs(seed: int = 0) -> dict:
    seeds = jax.random.split(jax.random.key(seed), 15)
    layer_input = normal_values(seeds[0], (TOKENS, D), 1.0, 6.0, ((0, 8),))
    positions = draw_positions(jax.random.fold_in(seeds[14], 71), 0)
    block_ids = draw_block_ids(jax.random.fold_in(seeds[14], 71), 0)
    ln_gain = jnp.clip(1.0 + 0.1 * jax.random.normal(seeds[3], (D,), jnp.float32), 0.5, 1.5)
    ln_bias = normal_values(seeds[4], (D,), 0.2, 1.0, (), jnp.float32)
    w_qkv = normal_values(seeds[5], (D, 3 * D), D ** -0.5, 0.1875, ((1, 4),))
    b_qkv = normal_values(seeds[6], (3 * D,), 0.2, 1.0, ((0, 4),), jnp.float32)
    w_dense = normal_values(seeds[7], (D, D), (D // 16) ** -0.5, 0.75, ((0, 4),))
    b_dense = normal_values(seeds[8], (D,), 0.2, 1.0, (), jnp.float32)
    w_in = normal_values(seeds[9], (D, FF), D ** -0.5, 0.1875, ((1, 4),))
    b_in = normal_values(seeds[10], (FF,), 0.2, 1.0, ((0, 4),), jnp.float32)
    w_out = normal_values(seeds[11], (FF, D), FF ** -0.5, 0.09375, ((0, 4),))
    b_out = normal_values(seeds[12], (D,), 0.2, 1.0, (), jnp.float32)
    cotangent = normal_values(seeds[13], (TOKENS, D), 1.0, 6.0, ((0, 8),))
    return dict(layer_input=layer_input, positions=positions, block_ids=block_ids, ln_gain=ln_gain, ln_bias=ln_bias, w_qkv=w_qkv, b_qkv=b_qkv, w_dense=w_dense, b_dense=b_dense, w_in=w_in, b_in=b_in, w_out=w_out, b_out=b_out, cotangent=cotangent)


@jax.custom_vjp
def low(v):
    return lax.optimization_barrier(v.astype(jnp.bfloat16)).astype(jnp.float32)

@jax.custom_vjp
def low_back(v):
    return v

def low_keep(v):
    return (low(v), None)

def low_pass(kept, grad):
    return (grad,)

def back_keep(v):
    return (v, None)

def back_low(kept, grad):
    return (low(grad),)
low.defvjp(low_keep, low_pass)
low_back.defvjp(back_keep, back_low)
eps = 1e-05
rotary_base = 10000.0

def angles(positions):
    frequency = rotary_base ** (-jnp.arange(0, ROT, 2).astype(jnp.float32) / ROT)
    phases = positions.astype(jnp.float32)[:, None] * frequency[None, :]
    phases = jnp.concatenate([phases, phases], axis=-1)
    return (jnp.cos(phases)[:, None, :], jnp.sin(phases)[:, None, :])

def rotate(source, cosine, sine_part):
    half_rot = ROT // 2
    rot_part = source[..., :ROT]
    turned = jnp.concatenate([-rot_part[..., half_rot:], rot_part[..., :half_rot]], axis=-1)
    return jnp.concatenate([rot_part * cosine + turned * sine_part, source[..., ROT:]], axis=-1)

def layer(input_seq, params, cosine, sine_part, blocks):
    gain, shift, w_qkv, b_qkv, w_dense, b_dense, w_in, b_in, w_out, b_out = params
    precise = lax.Precision.HIGHEST
    row_mean = lax.optimization_barrier(jnp.mean(input_seq, axis=-1, keepdims=True))
    centred = input_seq - row_mean
    variance = lax.optimization_barrier(jnp.mean(centred * centred, axis=-1, keepdims=True))
    normed = low(centred * lax.rsqrt(variance + eps) * gain + shift)
    projected = low_back(jnp.dot(normed, w_qkv, precision=precise) + b_qkv).reshape(SEQ, HEADS, 3, HD)
    query = low(rotate(projected[:, :, 0], cosine, sine_part))
    keys = low(rotate(projected[:, :, 1], cosine, sine_part))
    values = low(projected[:, :, 2])
    score_scale = HD ** (-0.5)

    def attend(block_item):
        query_block, block_row = block_item
        scores = low_back(jnp.einsum('qhd,khd->hqk', query_block, keys, precision=precise) * score_scale)
        allowed = blocks[None, None, :] <= block_row[None, :, None]
        scores = jnp.where(allowed, scores, -1e+30)
        row_max = lax.optimization_barrier(jnp.max(scores, axis=-1, keepdims=True))
        exp_scores = jnp.exp(scores - row_max)
        attn_prob = low(exp_scores / lax.optimization_barrier(jnp.sum(exp_scores, axis=-1, keepdims=True)))
        return jnp.einsum('hqk,khd->qhd', attn_prob, values, precision=precise)
    block_count = SEQ // QBLOCK
    mixed = lax.map(jax.checkpoint(attend), (query.reshape(block_count, QBLOCK, HEADS, HD), blocks.reshape(block_count, QBLOCK)))
    mixed = low(low_back(mixed.reshape(SEQ, D)))
    attn_branch = jnp.dot(mixed, w_dense, precision=precise) + b_dense
    hidden = low_back(jnp.dot(normed, w_in, precision=precise) + b_in)
    activated = low(jax.nn.gelu(hidden, approximate=False))
    mlp_branch = jnp.dot(activated, w_out, precision=precise) + b_out
    return input_seq + attn_branch + mlp_branch

def reference(layer_input, positions, block_ids, ln_gain, ln_bias, w_qkv, b_qkv, w_dense, b_dense, w_in, b_in, w_out, b_out, cotangent):
    params = tuple((item_array.astype(jnp.float32) for item_array in (ln_gain, ln_bias, w_qkv, b_qkv, w_dense, b_dense, w_in, b_in, w_out, b_out)))
    seq_count = TOKENS // SEQ
    input_seqs = layer_input.astype(jnp.float32).reshape(seq_count, SEQ, D)
    cot_seqs = cotangent.astype(jnp.float32).reshape(seq_count, SEQ, D)
    pos_seqs = positions.reshape(seq_count, SEQ)
    blk_seqs = block_ids.reshape(seq_count, SEQ)
    zeros = jax.tree.map(jnp.zeros_like, params)

    def per_sequence(summed, seq_item):
        input_seq, cot_seq, pos_seq, blk_seq = seq_item
        cosine, sine_part = angles(pos_seq)

        def forward(input_value, param_values):
            return layer(input_value, param_values, cosine, sine_part, blk_seq)
        result, pullback = jax.vjp(forward, input_seq, params)
        grad_x, grad_params = pullback(cot_seq)
        summed = jax.tree.map(lambda left, right: left + right, summed, grad_params)
        return (summed, (result.astype(jnp.bfloat16), grad_x))
    totals, (results, grads_x) = lax.scan(per_sequence, zeros, (input_seqs, cot_seqs, pos_seqs, blk_seqs))
    return (results.reshape(TOKENS, D), grads_x.reshape(TOKENS, D), totals[0], totals[1], totals[2], totals[3], totals[4], totals[5], totals[6], totals[7], totals[8], totals[9])
```

```python
import functools

import jax
import jax.numpy as jnp
import numpy as np
from jax import lax
from jax.experimental import pallas as pl
from jax.experimental.pallas import tpu as pltpu
from jax.sharding import PartitionSpec as P

HD = 64
ROT = 16
TILE = 256

eps = 1e-05
rotary_base = 10000.0
NT = (((1,), (1,)), ((), ()))
TN = (((0,), (0,)), ((), ()))
NN = (((1,), (0,)), ((), ()))


def mm(a, b, dims=NN):
    return lax.dot_general(a, b, dims, preferred_element_type=jnp.float32)


def lane_tables(positions):
    frequency = rotary_base ** (-jnp.arange(0, ROT, 2).astype(jnp.float32) / ROT)
    phases = positions.astype(jnp.float32)[:, None] * frequency[None, :]
    cosine, sine = jnp.cos(phases), jnp.sin(phases)
    tokens = positions.shape[0]
    ones = jnp.ones((tokens, HD - ROT), jnp.float32)
    none = jnp.zeros((tokens, HD - ROT), jnp.float32)
    half = jnp.zeros((tokens, ROT // 2), jnp.float32)
    cos_head = jnp.concatenate([cosine, cosine, ones], axis=1)
    low_head = jnp.concatenate([-sine, half, none], axis=1)
    high_head = jnp.concatenate([half, sine, none], axis=1)
    return tuple(jnp.concatenate([t, t], axis=1) for t in (cos_head, low_head, high_head))


def attention_kernel(
    heads,
    q,
    k,
    v,
    ids_col,
    ids_row,
    cot,
    normed,
    w_dense,
    w_qkv,
    perm,
    cos_t,
    low_t,
    high_t,
    row_mean,
    inv_std,
    x_hbm,
    mlp_hbm,
    dn_hbm,
    out_hbm,
    dnorm_hbm,
    gwd,
    gwqkv,
    gbqkv,
    gln,
    q_t,
    k_t,
    v_t,
    do,
    do_t,
    scores,
    probs,
    dscores,
    stack_a,
    stack_b,
    dk,
    dv,
    dq_t,
    mixed,
    lse,
    delta,
    dproj,
    stage_in,
    stage_x,
    stage_out,
    in_sem,
    x_sem,
    out_sem,
):
    tokens = q.shape[0]
    tiles = tokens // TILE
    width = heads * HD
    lane_head = lax.broadcasted_iota(jnp.int32, (1, width), 1) >> 6

    def head_lanes(h):
        return (lane_head == h).astype(jnp.float32).astype(jnp.bfloat16)

    row_head = lax.broadcasted_iota(jnp.int32, (width, 1), 0) >> 6

    def head_rows(h):
        return (row_head == h).astype(jnp.float32).astype(jnp.bfloat16)

    q_t[...] = q[...].T
    k_t[...] = k[...].T
    v_t[...] = v[...].T
    do[...] = mm(cot[...], w_dense[...], NT).astype(jnp.bfloat16)
    do_t[...] = do[...].T

    def load(hbm, buf, sem, t):
        copy = pltpu.make_async_copy(hbm.at[pl.ds(t * TILE, TILE)], buf, sem)
        copy.start()
        return copy

    def span(i):
        return min(i + 2, tiles) * TILE

    for i in range(tiles):
        fetch = load(mlp_hbm, stage_in, in_sem, i)
        n, cols = span(i), pl.ds(i * TILE, TILE)
        edge = pl.ds(i * TILE, n - i * TILE)

        def head_forward(h, _):
            rows = pl.ds(pl.multiple_of(h * HD, HD), HD)
            scores[0:n] = mm(k[0:n], q_t[:, cols] * head_rows(h))
            allowed = ids_col[edge, :] <= ids_row[:, cols]
            scores[edge] = jnp.where(allowed, scores[edge], -1e30)
            top = jnp.max(scores[0:n], axis=0, keepdims=True)
            weights = jnp.exp(scores[0:n] - top)
            total = jnp.sum(weights, axis=0, keepdims=True)
            probs[0:n, 0:TILE] = weights.astype(jnp.bfloat16)
            head_out = mm(v_t[rows, 0:n], probs[0:n, 0:TILE]) / total
            lse[pl.ds(h, 1), cols] = top + jnp.log(total)
            delta[pl.ds(h, 1), cols] = jnp.sum(
                head_out * do_t[rows, cols].astype(jnp.float32), axis=0, keepdims=True
            )
            dq_t[rows, cols] = head_out
            return 0

        lax.fori_loop(0, heads, head_forward, 0)
        mixed_tile = dq_t[:, cols].T.astype(jnp.bfloat16)
        mixed[cols] = mixed_tile
        if i:
            push.wait()
        fetch.wait()
        stage_out[...] = mm(mixed_tile, w_dense[...]) + stage_in[...]
        push = pltpu.make_async_copy(stage_out, out_hbm.at[cols], out_sem)
        push.start()

    gwd[...] = mm(mixed[...], cot[...], TN)

    def rotate_back(grad, rows):
        halves = []
        for part in range(width // 128):
            g = grad[:, part * 128 : (part + 1) * 128]
            halves.append(
                g * cos_t[rows]
                - pltpu.roll(g, 120, 1) * low_t[rows]
                - pltpu.roll(g, 8, 1) * high_t[rows]
            )
        return jnp.concatenate(halves, axis=1)

    def finish(t, push):
        rows = pl.ds(t * TILE, TILE)
        fetch = load(dn_hbm, stage_in, in_sem, t)
        fetch_x = load(x_hbm, stage_x, x_sem, t)
        dq_tile = rotate_back(dq_t[:, rows].T * (HD**-0.5), rows)
        dk_tile = rotate_back(dk[rows], rows)
        joined = jnp.concatenate([dq_tile, dk_tile, dv[rows]], axis=1).astype(jnp.bfloat16)
        laid = mm(joined, perm[...])
        dproj[rows] = laid.astype(jnp.bfloat16)
        gbqkv[...] += jnp.sum(laid, axis=0, keepdims=True)
        push.wait()
        fetch.wait()
        d_tile = mm(dproj[rows], w_qkv[...], NT) + stage_in[...]
        stage_out[...] = d_tile
        push = pltpu.make_async_copy(stage_out, dnorm_hbm.at[rows], out_sem)
        push.start()
        fetch_x.wait()
        standard = (stage_x[...].astype(jnp.float32) - row_mean[rows]) * inv_std[rows]
        gln[0:1] += jnp.sum(d_tile * standard, axis=0, keepdims=True)
        gln[1:2] += jnp.sum(d_tile, axis=0, keepdims=True)
        return push

    gbqkv[...] = jnp.zeros_like(gbqkv)
    gln[...] = jnp.zeros_like(gln)
    for i in reversed(range(tiles)):
        n, cols = span(i), pl.ds(i * TILE, TILE)
        edge = pl.ds(i * TILE, n - i * TILE)
        for h in range(heads):
            stack_a[h * TILE : (h + 1) * TILE] = do[cols] * head_lanes(h)
            stack_b[h * TILE : (h + 1) * TILE] = q[cols] * head_lanes(h)

        def head_backward(h, _):
            rows = pl.ds(pl.multiple_of(h * HD, HD), HD)
            block = pl.ds(pl.multiple_of(h * TILE, TILE), TILE)
            scores[0:n] = mm(k[0:n], q_t[:, cols] * head_rows(h))
            allowed = ids_col[edge, :] <= ids_row[:, cols]
            scores[edge] = jnp.where(allowed, scores[edge], -1e30)
            weights = jnp.exp(scores[0:n] - lse[pl.ds(h, 1), cols])
            probs[0:n, block] = weights.astype(jnp.bfloat16)
            d_weights = mm(v[0:n], do_t[:, cols] * head_rows(h))
            d_tile = weights * (d_weights - delta[pl.ds(h, 1), cols])
            dscores[0:n, block] = d_tile.astype(jnp.bfloat16)
            dq_t[rows, cols] = mm(k_t[rows, 0:n], dscores[0:n, block])
            return 0

        lax.fori_loop(0, heads, head_backward, 0)
        dv_part = mm(probs[0:n], stack_a[...])
        dk_part = mm(dscores[0:n], stack_b[...])
        if i == tiles - 1:
            dv[...] = dv_part
            dk[...] = dk_part
        else:
            dv[0:n] += dv_part
            dk[0:n] += dk_part
        if i < tiles - 1:
            push = finish(i + 1, push)
    push = finish(0, push)
    gwqkv[...] = mm(normed[...], dproj[...], TN)
    push.wait()


def attention(q, k, v, ids, cot, normed, w_dense, w_qkv, tables, row_mean, inv_std, x, mlp, dn):
    tokens, width = q.shape
    heads = width // HD
    d = x.shape[1]
    c = 3 * width
    order = np.arange(c).reshape(3, heads, HD).transpose(1, 0, 2).reshape(-1)
    perm = np.zeros((c, c), np.float32)
    perm[order, np.arange(c)] = 1.0
    vm = pl.BlockSpec(memory_space=pltpu.VMEM)
    hbm = pl.BlockSpec(memory_space=pl.ANY)
    f32, bf16 = jnp.float32, jnp.bfloat16
    scratch = [
        pltpu.VMEM((width, tokens), bf16),
        pltpu.VMEM((width, tokens), bf16),
        pltpu.VMEM((width, tokens), bf16),
        pltpu.VMEM((tokens, width), bf16),
        pltpu.VMEM((width, tokens), bf16),
        pltpu.VMEM((tokens, TILE), f32),
        pltpu.VMEM((tokens, heads * TILE), bf16),
        pltpu.VMEM((tokens, heads * TILE), bf16),
        pltpu.VMEM((heads * TILE, width), bf16),
        pltpu.VMEM((heads * TILE, width), bf16),
        pltpu.VMEM((tokens, width), f32),
        pltpu.VMEM((tokens, width), f32),
        pltpu.VMEM((width, tokens), f32),
        pltpu.VMEM((tokens, width), bf16),
        pltpu.VMEM((8, tokens), f32),
        pltpu.VMEM((8, tokens), f32),
        pltpu.VMEM((tokens, c), bf16),
        pltpu.VMEM((TILE, d), f32),
        pltpu.VMEM((TILE, d), bf16),
        pltpu.VMEM((TILE, d), f32),
        pltpu.SemaphoreType.DMA,
        pltpu.SemaphoreType.DMA,
        pltpu.SemaphoreType.DMA,
    ]
    return pl.pallas_call(
        functools.partial(attention_kernel, heads),
        out_shape=(
            jax.ShapeDtypeStruct((tokens, d), f32),
            jax.ShapeDtypeStruct((tokens, d), f32),
            jax.ShapeDtypeStruct((width, d), f32),
            jax.ShapeDtypeStruct((d, c), f32),
            jax.ShapeDtypeStruct((1, c), f32),
            jax.ShapeDtypeStruct((8, d), f32),
        ),
        in_specs=[vm] * 15 + [hbm] * 3,
        out_specs=(hbm, hbm, vm, vm, vm, vm),
        scratch_shapes=scratch,
        compiler_params=pltpu.CompilerParams(vmem_limit_bytes=60 << 20),
        name="attention",
    )(
        q,
        k,
        v,
        ids[:, None],
        ids[None, :],
        cot,
        normed,
        w_dense,
        w_qkv,
        jnp.asarray(perm, bf16),
        *tables,
        row_mean,
        inv_std,
        x,
        mlp,
        dn,
    )


def rotate(source, tables):
    tokens, width = source.shape
    cos_t, low_t, high_t = tables
    pairs = source.reshape(tokens, width // 128, 128)
    up = jnp.roll(pairs, -8, axis=2)
    down = jnp.roll(pairs, 8, axis=2)
    turned = pairs * cos_t[:, None] + up * low_t[:, None] + down * high_t[:, None]
    return turned.reshape(tokens, width)


def norm_back(d_rows, std_rows, inv_rows, cot_rows, gain):
    scaled = d_rows * gain
    inner = (
        scaled
        - jnp.mean(scaled, axis=-1, keepdims=True)
        - std_rows * jnp.mean(scaled * std_rows, axis=-1, keepdims=True)
    )
    return cot_rows + inv_rows * inner


def on_device(
    layer_input,
    positions,
    block_ids,
    ln_gain,
    ln_bias,
    w_qkv,
    b_qkv,
    w_dense,
    b_dense,
    w_in,
    b_in,
    w_out,
    b_out,
    cotangent,
):
    d = layer_input.shape[1]
    width = w_dense.shape[0]
    heads = width // HD
    input_float = layer_input.astype(jnp.float32)
    row_mean = jnp.mean(input_float, axis=-1, keepdims=True)
    centred = input_float - row_mean
    variance = jnp.mean(centred * centred, axis=-1, keepdims=True)
    inv_std = lax.rsqrt(variance + eps)
    standard = centred * inv_std
    normed = (standard * ln_gain + ln_bias).astype(jnp.bfloat16)
    tables = lane_tables(positions)
    w_parts = w_qkv.reshape(d, heads, 3, HD).transpose(2, 0, 1, 3).reshape(3, d, width)
    b_parts = b_qkv.reshape(heads, 3, HD).transpose(1, 0, 2).reshape(3, width)

    def project(part):
        return jnp.dot(normed, w_parts[part], preferred_element_type=jnp.float32) + b_parts[part]

    query = rotate(project(0), tables).astype(jnp.bfloat16) * jnp.bfloat16(HD**-0.5)
    keys = rotate(project(1), tables).astype(jnp.bfloat16)
    values = project(2).astype(jnp.bfloat16)

    hidden = jnp.dot(normed, w_in, preferred_element_type=jnp.float32) + b_in
    normal_cdf = 0.5 * (1.0 + lax.erf(hidden * 0.7071067811865476))
    activated = (hidden * normal_cdf).astype(jnp.bfloat16)
    mlp_part = jnp.dot(activated, w_out, preferred_element_type=jnp.float32)
    cot_float = cotangent.astype(jnp.float32)
    bias_grad = jnp.sum(cot_float, axis=0)
    grad_w_out = jnp.einsum("tf,td->fd", activated, cotangent, preferred_element_type=jnp.float32)
    d_activated = jnp.dot(cotangent, w_out.T, preferred_element_type=jnp.float32)
    normal_pdf = jnp.exp(-0.5 * hidden * hidden) * 0.3989422804014327
    d_hidden = (d_activated * (normal_cdf + hidden * normal_pdf)).astype(jnp.bfloat16)
    grad_w_in = jnp.einsum("td,tf->df", normed, d_hidden, preferred_element_type=jnp.float32)
    grad_b_in = jnp.sum(d_hidden, axis=0, dtype=jnp.float32)
    d_mlp = jnp.dot(d_hidden, w_in.T, preferred_element_type=jnp.float32)

    branch, d_normed, grad_w_dense, grad_w_qkv, grad_b_qkv, grad_ln = attention(
        query,
        keys,
        values,
        block_ids,
        cotangent,
        normed,
        w_dense,
        w_qkv,
        tables,
        row_mean,
        inv_std,
        layer_input,
        mlp_part,
        d_mlp,
    )
    branches, d_full = lax.psum((branch, d_normed), "tensor")
    output = (input_float + branches + b_dense + b_out).astype(jnp.bfloat16)
    grad_input = norm_back(d_full, standard, inv_std, cot_float, ln_gain)
    grad_gain, grad_shift = lax.psum((grad_ln[0], grad_ln[1]), ("dp", "tensor"))
    (
        grad_w_qkv,
        grad_b_qkv,
        grad_w_dense,
        bias_grad,
        grad_w_in,
        grad_b_in,
        grad_w_out,
    ) = lax.psum(
        (
            grad_w_qkv,
            grad_b_qkv[0],
            grad_w_dense,
            bias_grad,
            grad_w_in,
            grad_b_in,
            grad_w_out,
        ),
        "dp",
    )
    return (
        output,
        grad_input,
        grad_gain,
        grad_shift,
        grad_w_qkv,
        grad_b_qkv,
        grad_w_dense,
        bias_grad,
        grad_w_in,
        grad_b_in,
        grad_w_out,
        bias_grad,
    )


def solution(mesh):
    in_specs = (
        P("dp", None),
        P("dp"),
        P("dp"),
        P(),
        P(),
        P(None, "tensor"),
        P("tensor"),
        P("tensor", None),
        P(),
        P(None, "tensor"),
        P("tensor"),
        P("tensor", None),
        P(),
        P("dp", None),
    )
    out_specs = (
        P("dp", None),
        P("dp", None),
        P(),
        P(),
        P(None, "tensor"),
        P("tensor"),
        P("tensor", None),
        P(),
        P(None, "tensor"),
        P("tensor"),
        P("tensor", None),
        P(),
    )
    return jax.shard_map(
        on_device, mesh=mesh, in_specs=in_specs, out_specs=out_specs, check_vma=False
    )
```

```python
import functools

import jax
import jax.numpy as jnp
import numpy as np
from jax import lax
from jax.experimental import pallas as pl
from jax.experimental.pallas import tpu as pltpu
from jax.sharding import PartitionSpec as P

HD = 64
ROT = 16
TILE = 256

eps = 1e-05
rotary_base = 10000.0
NT = (((1,), (1,)), ((), ()))
TN = (((0,), (0,)), ((), ()))
NN = (((1,), (0,)), ((), ()))


def mm(a, b, dims=NN):
    return lax.dot_general(a, b, dims, preferred_element_type=jnp.float32)


def lane_tables(positions):
    frequency = rotary_base ** (-jnp.arange(0, ROT, 2).astype(jnp.float32) / ROT)
    phases = positions.astype(jnp.float32)[:, None] * frequency[None, :]
    cosine, sine = jnp.cos(phases), jnp.sin(phases)
    tokens = positions.shape[0]
    ones = jnp.ones((tokens, HD - ROT), jnp.float32)
    none = jnp.zeros((tokens, HD - ROT), jnp.float32)
    half = jnp.zeros((tokens, ROT // 2), jnp.float32)
    cos_head = jnp.concatenate([cosine, cosine, ones], axis=1)
    low_head = jnp.concatenate([-sine, half, none], axis=1)
    high_head = jnp.concatenate([half, sine, none], axis=1)
    return tuple(jnp.concatenate([t, t], axis=1) for t in (cos_head, low_head, high_head))


def attention_kernel(
    heads,
    q,
    k,
    v,
    ids_col,
    ids_row,
    cot,
    normed,
    w_dense,
    w_qkv,
    perm,
    cos_t,
    low_t,
    high_t,
    row_mean,
    inv_std,
    x_hbm,
    mlp_hbm,
    dn_hbm,
    out_hbm,
    dnorm_hbm,
    gwd,
    gwqkv,
    gbqkv,
    gln,
    q_t,
    k_t,
    v_t,
    do,
    do_t,
    scores,
    probs,
    dscores,
    stack_a,
    stack_b,
    dk,
    dv,
    dq_t,
    mixed,
    lse,
    delta,
    dproj,
    stage_in,
    stage_x,
    stage_out,
    in_sem,
    x_sem,
    out_sem,
):
    tokens = q.shape[0]
    tiles = tokens // TILE
    width = heads * HD
    lane_head = lax.broadcasted_iota(jnp.int32, (1, width), 1) >> 6

    def head_lanes(h):
        return (lane_head == h).astype(jnp.float32).astype(jnp.bfloat16)

    row_head = lax.broadcasted_iota(jnp.int32, (width, 1), 0) >> 6

    def head_rows(h):
        return (row_head == h).astype(jnp.float32).astype(jnp.bfloat16)

    q_t[...] = q[...].T
    k_t[...] = k[...].T
    v_t[...] = v[...].T
    do[...] = mm(cot[...], w_dense[...], NT).astype(jnp.bfloat16)
    do_t[...] = do[...].T

    def load(hbm, buf, sem, t):
        copy = pltpu.make_async_copy(hbm.at[pl.ds(t * TILE, TILE)], buf, sem)
        copy.start()
        return copy

    def span(i):
        return min(i + 2, tiles) * TILE

    for i in range(tiles):
        fetch = load(mlp_hbm, stage_in, in_sem, i)
        n, cols = span(i), pl.ds(i * TILE, TILE)
        edge = pl.ds(i * TILE, n - i * TILE)

        def head_forward(h, _):
            rows = pl.ds(pl.multiple_of(h * HD, HD), HD)
            scores[0:n] = mm(k[0:n], q_t[:, cols] * head_rows(h))
            allowed = ids_col[edge, :] <= ids_row[:, cols]
            scores[edge] = jnp.where(allowed, scores[edge], -1e30)
            top = jnp.max(scores[0:n], axis=0, keepdims=True)
            weights = jnp.exp(scores[0:n] - top)
            total = jnp.sum(weights, axis=0, keepdims=True)
            probs[0:n, 0:TILE] = weights.astype(jnp.bfloat16)
            head_out = mm(v_t[rows, 0:n], probs[0:n, 0:TILE]) / total
            lse[pl.ds(h, 1), cols] = top + jnp.log(total)
            delta[pl.ds(h, 1), cols] = jnp.sum(
                head_out * do_t[rows, cols].astype(jnp.float32), axis=0, keepdims=True
            )
            dq_t[rows, cols] = head_out
            return 0

        lax.fori_loop(0, heads, head_forward, 0)
        mixed_tile = dq_t[:, cols].T.astype(jnp.bfloat16)
        mixed[cols] = mixed_tile
        if i:
            push.wait()
        fetch.wait()
        stage_out[...] = mm(mixed_tile, w_dense[...]) + stage_in[...]
        push = pltpu.make_async_copy(stage_out, out_hbm.at[cols], out_sem)
        push.start()

    gwd[...] = mm(mixed[...], cot[...], TN)

    def rotate_back(grad, rows):
        halves = []
        for part in range(width // 128):
            g = grad[:, part * 128 : (part + 1) * 128]
            halves.append(
                g * cos_t[rows]
                - pltpu.roll(g, 120, 1) * low_t[rows]
                - pltpu.roll(g, 8, 1) * high_t[rows]
            )
        return jnp.concatenate(halves, axis=1)

    def finish(t, push):
        rows = pl.ds(t * TILE, TILE)
        fetch = load(dn_hbm, stage_in, in_sem, t)
        fetch_x = load(x_hbm, stage_x, x_sem, t)
        dq_tile = rotate_back(dq_t[:, rows].T * (HD**-0.5), rows)
        dk_tile = rotate_back(dk[rows], rows)
        joined = jnp.concatenate([dq_tile, dk_tile, dv[rows]], axis=1).astype(jnp.bfloat16)
        laid = mm(joined, perm[...])
        dproj[rows] = laid.astype(jnp.bfloat16)
        gbqkv[...] += jnp.sum(laid, axis=0, keepdims=True)
        push.wait()
        fetch.wait()
        d_tile = mm(dproj[rows], w_qkv[...], NT) + stage_in[...]
        stage_out[...] = d_tile
        push = pltpu.make_async_copy(stage_out, dnorm_hbm.at[rows], out_sem)
        push.start()
        fetch_x.wait()
        standard = (stage_x[...].astype(jnp.float32) - row_mean[rows]) * inv_std[rows]
        gln[0:1] += jnp.sum(d_tile * standard, axis=0, keepdims=True)
        gln[1:2] += jnp.sum(d_tile, axis=0, keepdims=True)
        return push

    gbqkv[...] = jnp.zeros_like(gbqkv)
    gln[...] = jnp.zeros_like(gln)
    for i in reversed(range(tiles)):
        n, cols = span(i), pl.ds(i * TILE, TILE)
        edge = pl.ds(i * TILE, n - i * TILE)
        for h in range(heads):
            stack_a[h * TILE : (h + 1) * TILE] = do[cols] * head_lanes(h)
            stack_b[h * TILE : (h + 1) * TILE] = q[cols] * head_lanes(h)

        def head_backward(h, _):
            rows = pl.ds(pl.multiple_of(h * HD, HD), HD)
            block = pl.ds(pl.multiple_of(h * TILE, TILE), TILE)
            scores[0:n] = mm(k[0:n], q_t[:, cols] * head_rows(h))
            allowed = ids_col[edge, :] <= ids_row[:, cols]
            scores[edge] = jnp.where(allowed, scores[edge], -1e30)
            weights = jnp.exp(scores[0:n] - lse[pl.ds(h, 1), cols])
            probs[0:n, block] = weights.astype(jnp.bfloat16)
            d_weights = mm(v[0:n], do_t[:, cols] * head_rows(h))
            d_tile = weights * (d_weights - delta[pl.ds(h, 1), cols])
            dscores[0:n, block] = d_tile.astype(jnp.bfloat16)
            dq_t[rows, cols] = mm(k_t[rows, 0:n], dscores[0:n, block])
            return 0

        lax.fori_loop(0, heads, head_backward, 0)
        dv_part = mm(probs[0:n], stack_a[...])
        dk_part = mm(dscores[0:n], stack_b[...])
        if i == tiles - 1:
            dv[...] = dv_part
            dk[...] = dk_part
        else:
            dv[0:n] += dv_part
            dk[0:n] += dk_part
        if i < tiles - 1:
            push = finish(i + 1, push)
    push = finish(0, push)
    gwqkv[...] = mm(normed[...], dproj[...], TN)
    push.wait()


def attention(q, k, v, ids, cot, normed, w_dense, w_qkv, tables, row_mean, inv_std, x, mlp, dn):
    tokens, width = q.shape
    heads = width // HD
    d = x.shape[1]
    c = 3 * width
    order = np.arange(c).reshape(3, heads, HD).transpose(1, 0, 2).reshape(-1)
    perm = np.zeros((c, c), np.float32)
    perm[order, np.arange(c)] = 1.0
    vm = pl.BlockSpec(memory_space=pltpu.VMEM)
    hbm = pl.BlockSpec(memory_space=pl.ANY)
    f32, bf16 = jnp.float32, jnp.bfloat16
    scratch = [
        pltpu.VMEM((width, tokens), bf16),
        pltpu.VMEM((width, tokens), bf16),
        pltpu.VMEM((width, tokens), bf16),
        pltpu.VMEM((tokens, width), bf16),
        pltpu.VMEM((width, tokens), bf16),
        pltpu.VMEM((tokens, TILE), f32),
        pltpu.VMEM((tokens, heads * TILE), bf16),
        pltpu.VMEM((tokens, heads * TILE), bf16),
        pltpu.VMEM((heads * TILE, width), bf16),
        pltpu.VMEM((heads * TILE, width), bf16),
        pltpu.VMEM((tokens, width), f32),
        pltpu.VMEM((tokens, width), f32),
        pltpu.VMEM((width, tokens), f32),
        pltpu.VMEM((tokens, width), bf16),
        pltpu.VMEM((8, tokens), f32),
        pltpu.VMEM((8, tokens), f32),
        pltpu.VMEM((tokens, c), bf16),
        pltpu.VMEM((TILE, d), f32),
        pltpu.VMEM((TILE, d), bf16),
        pltpu.VMEM((TILE, d), f32),
        pltpu.SemaphoreType.DMA,
        pltpu.SemaphoreType.DMA,
        pltpu.SemaphoreType.DMA,
    ]
    return pl.pallas_call(
        functools.partial(attention_kernel, heads),
        out_shape=(
            jax.ShapeDtypeStruct((tokens, d), f32),
            jax.ShapeDtypeStruct((tokens, d), f32),
            jax.ShapeDtypeStruct((width, d), f32),
            jax.ShapeDtypeStruct((d, c), f32),
            jax.ShapeDtypeStruct((1, c), f32),
            jax.ShapeDtypeStruct((8, d), f32),
        ),
        in_specs=[vm] * 15 + [hbm] * 3,
        out_specs=(hbm, hbm, vm, vm, vm, vm),
        scratch_shapes=scratch,
        compiler_params=pltpu.CompilerParams(vmem_limit_bytes=60 << 20),
        name="attention",
    )(
        q,
        k,
        v,
        ids[:, None],
        ids[None, :],
        cot,
        normed,
        w_dense,
        w_qkv,
        jnp.asarray(perm, bf16),
        *tables,
        row_mean,
        inv_std,
        x,
        mlp,
        dn,
    )


SLOTS = 5
STAGES = 6
CHUNK = 64
MESH_ID = pl.DeviceIdType.MESH


def z_stride(group):
    return 2 if group == 8 else 4


class Peers:
    def __init__(self, dp_size):
        stride = z_stride(dp_size)
        d, t = lax.axis_index("dp"), lax.axis_index("tensor")
        z = lax.rem(lax.div(d, stride), 4)
        base = d - z * stride
        self.y_half = lax.rem(d, 2)
        self.z_half = lax.div(z, 2)
        self.middle = jnp.logical_or(z == 1, z == 2)
        self.end = jnp.logical_or(z == 0, z == 3)
        self.y = (d + 1 - 2 * self.y_half, t)
        self.z_pair = (base + stride * (z + 1 - 2 * lax.rem(z, 2)), t)
        self.z_mid = (base + stride * (3 - z), t)
        self.z_far = (base + stride * lax.rem(z + 2, 4), t)
        self.core = (d, t + 1 - 2 * lax.rem(t, 2))
        self.x = (d, lax.rem(t + 2, 4))

    def greet(self):
        barrier = pltpu.get_barrier_semaphore()
        partners = (self.y, self.z_pair, self.z_mid, self.z_far, self.core, self.x)
        for partner in partners:
            pl.semaphore_signal(barrier, inc=1, device_id=partner, device_id_type=MESH_ID)
        pl.semaphore_wait(barrier, len(partners))


def remote(src, dst, sems, index, device):
    return pltpu.make_async_remote_copy(
        src_ref=src,
        dst_ref=dst,
        send_sem=sems.at[(0,) + index],
        recv_sem=sems.at[(1,) + index],
        device_id=device,
        device_id_type=MESH_ID,
    )


class LineFirst:
    def __init__(self, peers, chunks, scratch):
        self.p, self.chunks = peers, chunks
        self.land, self.work, self.mid, self.side, self.done, self.sems, self.local = scratch

    @staticmethod
    def scratch():
        f32 = jnp.float32
        return [
            pltpu.VMEM((SLOTS, CHUNK, 1024), f32),
            pltpu.VMEM((SLOTS, CHUNK, 1024), f32),
            pltpu.VMEM((SLOTS, CHUNK // 2, 1024), f32),
            pltpu.VMEM((SLOTS, CHUNK // 2, 1024), f32),
            pltpu.VMEM((SLOTS, CHUNK, 1024), f32),
            pltpu.SemaphoreType.DMA((2, 5, SLOTS)),
            pltpu.SemaphoreType.DMA((2, SLOTS)),
        ]

    def stage(self, c, s):
        p, slot = self.p, c % SLOTS
        part, total, row, cols = self.chunks[c]
        rows, lanes = pl.ds(row, CHUNK), pl.ds(0, cols)
        half = CHUNK // 2
        own = pl.ds(pl.multiple_of(p.z_half * half, half), half)
        other = pl.ds(pl.multiple_of((1 - p.z_half) * half, half), half)
        land, work = self.land.at[slot, :, lanes], self.work.at[slot, :, lanes]
        mid, side = self.mid.at[slot, :, lanes], self.side.at[slot, :, lanes]
        done = self.done.at[slot, :, lanes]
        inward = functools.partial(remote, part.at[rows], land, self.sems, (0, slot), p.z_pair)
        across = functools.partial(remote, work.at[other], mid, self.sems, (1, slot), p.z_mid)
        beside = functools.partial(remote, work.at[own], side, self.sems, (2, slot), p.y)
        back = functools.partial(remote, done.at[own], done.at[own], self.sems, (3, slot), p.z_mid)
        outward = functools.partial(remote, done, total.at[rows], self.sems, (4, slot), p.z_pair)
        fetch = functools.partial(pltpu.make_async_copy, part.at[rows], work, self.local.at[0, slot])
        store = functools.partial(pltpu.make_async_copy, done, total.at[rows], self.local.at[1, slot])

        if s == 0:

            @pl.when(p.end)
            def _():
                inward().start()

            @pl.when(p.middle)
            def _():
                fetch().start()

        if s == 5:

            @pl.when(p.end)
            def _():
                outward().wait_recv()
                inward().wait_send()

        if s > 0:

            @pl.when(p.middle)
            def _():
                if s == 1:
                    fetch().wait()
                    inward().wait_recv()
                    work[...] += land[...]
                    across().start()
                if s == 2:
                    across().wait_recv()
                    work[own] += mid[...]
                    beside().start()
                if s == 3:
                    beside().wait_recv()
                    done[own] = work[own] + side[...]
                    back().start()
                if s == 4:
                    back().wait_recv()
                    outward().start()
                    store().start()
                if s == 5:
                    for copy in (across, beside, back, outward):
                        copy().wait_send()
                    store().wait()

    def tick(self, t):
        for s in reversed(range(STAGES)):
            if 0 <= t - s < len(self.chunks):
                self.stage(t - s, s)


class SideFirst:
    def __init__(self, peers, chunks, scratch):
        self.p, self.chunks = peers, chunks
        self.land, self.work, self.line, self.mid, self.done, self.sems, self.local = scratch

    @staticmethod
    def scratch():
        return [pltpu.VMEM((SLOTS, CHUNK // 2, 1024), jnp.float32)] * 5 + [
            pltpu.SemaphoreType.DMA((2, 5, SLOTS)),
            pltpu.SemaphoreType.DMA((2, SLOTS)),
        ]

    def stage(self, c, s):
        p, slot = self.p, c % SLOTS
        part, total, row, cols = self.chunks[c]
        lanes, half = pl.ds(0, cols), CHUNK // 2
        own = pl.ds(pl.multiple_of(row + p.y_half * half, half), half)
        other = pl.ds(pl.multiple_of(row + (1 - p.y_half) * half, half), half)
        land, work = self.land.at[slot, :, lanes], self.work.at[slot, :, lanes]
        line, mid = self.line.at[slot, :, lanes], self.mid.at[slot, :, lanes]
        done = self.done.at[slot, :, lanes]
        beside = functools.partial(remote, part.at[other], land, self.sems, (0, slot), p.y)
        inward = functools.partial(remote, work, line, self.sems, (1, slot), p.z_pair)
        across = functools.partial(remote, work, mid, self.sems, (2, slot), p.z_mid)
        outward = functools.partial(remote, done, done, self.sems, (3, slot), p.z_pair)
        back = functools.partial(remote, done, total.at[own], self.sems, (4, slot), p.y)
        fetch = functools.partial(pltpu.make_async_copy, part.at[own], work, self.local.at[0, slot])
        store = functools.partial(pltpu.make_async_copy, done, total.at[own], self.local.at[1, slot])

        if s == 0:
            beside().start()
            fetch().start()
        if s == 1:
            fetch().wait()
            beside().wait_recv()
            work[...] += land[...]

            @pl.when(p.end)
            def _():
                inward().start()

        if s in (2, 3):

            @pl.when(p.middle)
            def _():
                if s == 2:
                    inward().wait_recv()
                    work[...] += line[...]
                    across().start()
                if s == 3:
                    across().wait_recv()
                    done[...] = work[...] + mid[...]
                    outward().start()

        if s == 4:

            @pl.when(p.end)
            def _():
                outward().wait_recv()

            back().start()
            store().start()
        if s == 5:
            back().wait()
            beside().wait_send()
            store().wait()

            @pl.when(p.end)
            def _():
                inward().wait_send()

            @pl.when(p.middle)
            def _():
                across().wait_send()
                outward().wait_send()

    def tick(self, t):
        for s in reversed(range(STAGES)):
            if 0 <= t - s < len(self.chunks):
                self.stage(t - s, s)


class SmallSum:
    def __init__(self, peers, scratch):
        self.p = peers
        self.kept, self.got, self.sems = scratch

    @staticmethod
    def scratch():
        return [
            pltpu.VMEM((6, 8, 1024), jnp.float32),
            pltpu.VMEM((5, 8, 1024), jnp.float32),
            pltpu.SemaphoreType.DMA((2, 5)),
        ]

    def copy(self, s):
        p = self.p
        partner = (p.y, p.z_pair, p.z_far, p.core, p.x)[s]
        return remote(self.kept.at[s], self.got.at[s], self.sems, (s,), partner)

    def start(self, rows):
        self.kept[0] = rows
        self.copy(0).start()

    def step(self, s):
        self.copy(s).wait()
        self.kept[s + 1] = self.kept[s] + self.got[s]
        if s < 4:
            self.copy(s + 1).start()


def chunk_lists(parts, totals):
    ways = ([], [])
    for turn, (part, total) in enumerate(zip(parts, totals)):
        for i in range(part.shape[0] // CHUNK):
            ways[(turn if turn < 2 else i) % 2].append((part, total, i * CHUNK, part.shape[1]))
    return ways


def sums_kernel(dp_size, w_out, w_in, w_dense, w_qkv, small, *rest):
    totals, small_total, scratch = rest[:4], rest[4], rest[5:]
    peers = Peers(dp_size)
    peers.greet()
    line, side = chunk_lists((w_out, w_in, w_dense, w_qkv), totals)
    first = LineFirst(peers, line, scratch[:7])
    second = SideFirst(peers, side, scratch[7:14])
    little = SmallSum(peers, scratch[14:])
    little.start(small[...])
    for t in range(max(len(line), len(side)) + STAGES - 1):
        first.tick(t)
        second.tick(t)
        if t < 5:
            little.step(t)
            if t == 2:
                small_total[0:8] = little.kept[3]
            if t == 4:
                small_total[8:16] = little.kept[5]


def group_sums(dp_size, parts, small):
    vm = pl.BlockSpec(memory_space=pltpu.VMEM)
    hbm = pl.BlockSpec(memory_space=pl.ANY)
    outs = [jax.ShapeDtypeStruct(p.shape, jnp.float32) for p in parts]
    return pl.pallas_call(
        functools.partial(sums_kernel, dp_size),
        out_shape=tuple(outs) + (jax.ShapeDtypeStruct((16, 1024), jnp.float32),),
        in_specs=[hbm] * 4 + [vm],
        out_specs=tuple([hbm] * 4 + [vm]),
        scratch_shapes=LineFirst.scratch() + SideFirst.scratch() + SmallSum.scratch(),
        compiler_params=pltpu.CompilerParams(
            collective_id=0, has_side_effects=True, vmem_limit_bytes=40 << 20
        ),
        name="group_sums",
    )(*parts, small)


def rest_groups(dp_size):
    stride = z_stride(dp_size)
    places = np.arange(dp_size).reshape(-1, 4, stride // 2, 2)
    return places.transpose(1, 3, 0, 2).reshape(8, -1).tolist()


def rotate(source, tables):
    tokens, width = source.shape
    cos_t, low_t, high_t = tables
    pairs = source.reshape(tokens, width // 128, 128)
    up = jnp.roll(pairs, -8, axis=2)
    down = jnp.roll(pairs, 8, axis=2)
    turned = pairs * cos_t[:, None] + up * low_t[:, None] + down * high_t[:, None]
    return turned.reshape(tokens, width)


def norm_back(d_rows, std_rows, inv_rows, cot_rows, gain):
    scaled = d_rows * gain
    inner = (
        scaled
        - jnp.mean(scaled, axis=-1, keepdims=True)
        - std_rows * jnp.mean(scaled * std_rows, axis=-1, keepdims=True)
    )
    return cot_rows + inv_rows * inner


def on_device(
    dp_size,
    layer_input,
    positions,
    block_ids,
    ln_gain,
    ln_bias,
    w_qkv,
    b_qkv,
    w_dense,
    b_dense,
    w_in,
    b_in,
    w_out,
    b_out,
    cotangent,
):
    d = layer_input.shape[1]
    width = w_dense.shape[0]
    heads = width // HD
    input_float = layer_input.astype(jnp.float32)
    row_mean = jnp.mean(input_float, axis=-1, keepdims=True)
    centred = input_float - row_mean
    variance = jnp.mean(centred * centred, axis=-1, keepdims=True)
    inv_std = lax.rsqrt(variance + eps)
    standard = centred * inv_std
    normed = (standard * ln_gain + ln_bias).astype(jnp.bfloat16)
    tables = lane_tables(positions)
    w_parts = w_qkv.reshape(d, heads, 3, HD).transpose(2, 0, 1, 3).reshape(3, d, width)
    b_parts = b_qkv.reshape(heads, 3, HD).transpose(1, 0, 2).reshape(3, width)

    def project(part):
        return jnp.dot(normed, w_parts[part], preferred_element_type=jnp.float32) + b_parts[part]

    query = rotate(project(0), tables).astype(jnp.bfloat16) * jnp.bfloat16(HD**-0.5)
    keys = rotate(project(1), tables).astype(jnp.bfloat16)
    values = project(2).astype(jnp.bfloat16)

    hidden = jnp.dot(normed, w_in, preferred_element_type=jnp.float32) + b_in
    normal_cdf = 0.5 * (1.0 + lax.erf(hidden * 0.7071067811865476))
    activated = (hidden * normal_cdf).astype(jnp.bfloat16)
    mlp_part = jnp.dot(activated, w_out, preferred_element_type=jnp.float32)
    cot_float = cotangent.astype(jnp.float32)
    bias_grad = jnp.sum(cot_float, axis=0)
    grad_w_out = jnp.einsum("tf,td->fd", activated, cotangent, preferred_element_type=jnp.float32)
    d_activated = jnp.dot(cotangent, w_out.T, preferred_element_type=jnp.float32)
    normal_pdf = jnp.exp(-0.5 * hidden * hidden) * 0.3989422804014327
    d_hidden = (d_activated * (normal_cdf + hidden * normal_pdf)).astype(jnp.bfloat16)
    grad_w_in = jnp.einsum("td,tf->df", normed, d_hidden, preferred_element_type=jnp.float32)
    grad_b_in = jnp.sum(d_hidden, axis=0, dtype=jnp.float32)
    d_mlp = jnp.dot(d_hidden, w_in.T, preferred_element_type=jnp.float32)

    branch, d_normed, grad_w_dense, grad_w_qkv, grad_b_qkv, grad_ln = attention(
        query,
        keys,
        values,
        block_ids,
        cotangent,
        normed,
        w_dense,
        w_qkv,
        tables,
        row_mean,
        inv_std,
        layer_input,
        mlp_part,
        d_mlp,
    )
    branches, d_full = lax.psum((branch, d_normed), "tensor")
    output = (input_float + branches + b_dense + b_out).astype(jnp.bfloat16)
    grad_input = norm_back(d_full, standard, inv_std, cot_float, ln_gain)
    pad = jnp.zeros((1024 - 3 * width,), jnp.float32)
    small = jnp.stack(
        [grad_ln[0], grad_ln[1], bias_grad, grad_b_in, jnp.concatenate([grad_b_qkv[0], pad])]
        + [jnp.zeros((d,), jnp.float32)] * 3
    )
    sums = group_sums(dp_size, (grad_w_out, grad_w_in, grad_w_dense, grad_w_qkv), small)
    if dp_size > 8:
        sums = lax.psum(sums, "dp", axis_index_groups=rest_groups(dp_size))
    grad_w_out, grad_w_in, grad_w_dense, grad_w_qkv, small = sums
    bias_grad, grad_b_in, grad_b_qkv = small[2], small[3], small[4, : 3 * width]
    grad_gain, grad_shift = small[8], small[9]
    return (
        output,
        grad_input,
        grad_gain,
        grad_shift,
        grad_w_qkv,
        grad_b_qkv,
        grad_w_dense,
        bias_grad,
        grad_w_in,
        grad_b_in,
        grad_w_out,
        bias_grad,
    )


def solution(mesh):
    in_specs = (
        P("dp", None),
        P("dp"),
        P("dp"),
        P(),
        P(),
        P(None, "tensor"),
        P("tensor"),
        P("tensor", None),
        P(),
        P(None, "tensor"),
        P("tensor"),
        P("tensor", None),
        P(),
        P("dp", None),
    )
    out_specs = (
        P("dp", None),
        P("dp", None),
        P(),
        P(),
        P(None, "tensor"),
        P("tensor"),
        P("tensor", None),
        P(),
        P(None, "tensor"),
        P("tensor"),
        P("tensor", None),
        P(),
    )
    return jax.shard_map(
        functools.partial(on_device, mesh.shape["dp"]), mesh=mesh, in_specs=in_specs, out_specs=out_specs, check_vma=False
    )
```

```python
import functools

import jax
import jax.numpy as jnp
import numpy as np
from jax import lax
from jax.experimental import pallas as pl
from jax.experimental.pallas import tpu as pltpu
from jax.sharding import PartitionSpec as P

HD = 64
ROT = 16
TILE = 256

eps = 1e-05
rotary_base = 10000.0
NT = (((1,), (1,)), ((), ()))
TN = (((0,), (0,)), ((), ()))
NN = (((1,), (0,)), ((), ()))


def mm(a, b, dims=NN):
    return lax.dot_general(a, b, dims, preferred_element_type=jnp.float32)


def lane_tables(positions):
    frequency = rotary_base ** (-jnp.arange(0, ROT, 2).astype(jnp.float32) / ROT)
    phases = positions.astype(jnp.float32)[:, None] * frequency[None, :]
    cosine, sine = jnp.cos(phases), jnp.sin(phases)
    tokens = positions.shape[0]
    ones = jnp.ones((tokens, HD - ROT), jnp.float32)
    none = jnp.zeros((tokens, HD - ROT), jnp.float32)
    half = jnp.zeros((tokens, ROT // 2), jnp.float32)
    cos_head = jnp.concatenate([cosine, cosine, ones], axis=1)
    low_head = jnp.concatenate([-sine, half, none], axis=1)
    high_head = jnp.concatenate([half, sine, none], axis=1)
    return tuple(jnp.concatenate([t, t], axis=1) for t in (cos_head, low_head, high_head))


def attention_kernel(
    heads,
    dp_size,
    q,
    k,
    v,
    ids_col,
    ids_row,
    w_dense,
    w_qkv,
    perm,
    small,
    cot_hbm,
    normed_hbm,
    tables_hbm,
    x_hbm,
    mlp_hbm,
    dn_hbm,
    gw_out,
    gw_in,
    out_sum,
    dnorm_sum,
    sum_w_out,
    sum_w_in,
    sum_w_dense,
    sum_w_qkv,
    small_sum,
    out_part,
    dnorm_part,
    gw_dense,
    gw_qkv,
    q_t,
    k_t,
    v_t,
    do,
    do_t,
    scores,
    probs,
    dscores,
    stack_a,
    stack_b,
    dk,
    dv,
    dq_t,
    mixed,
    lse,
    delta,
    dproj,
    wide,
    rows_sum,
    stage_in,
    stage_x,
    stage_t,
    stage_out,
    stage_w,
    in_sem,
    x_sem,
    t_sem,
    out_sem,
    w_sem,
    wide_sem,
    *comm,
):
    tokens, d = x_hbm.shape
    tiles = tokens // TILE
    width = heads * HD
    parts = len(LineFirst.scratch())
    peers = Peers(dp_size)
    line, side = chunk_lists(
        (gw_out, gw_in, gw_dense, gw_qkv), (sum_w_out, sum_w_in, sum_w_dense, sum_w_qkv)
    )
    line_sum = LineFirst(peers, line, comm[:parts])
    side_sum = SideFirst(peers, side, comm[parts : 2 * parts])
    little = SmallSum(peers, comm[2 * parts : 2 * parts + 3])
    tensor_sum = TensorSum(
        peers,
        [(out_part, out_sum, t * TILE) for t in range(tiles)]
        + [(dnorm_part, dnorm_sum, t * TILE) for t in reversed(range(tiles))],
        comm[2 * parts + 3 :],
    )
    state = {"d": 0, "x": 0, "made": 0, "owed": 0.0, "push": None}

    def settle():
        if state["push"] is not None:
            state["push"].wait()
            state["push"] = None

    def tick_x():
        n = state["x"]
        if n < len(tensor_sum.chunks) + 3 and (n < state["made"] or n >= len(tensor_sum.chunks)):
            settle()
            tensor_sum.tick(n)
            state["x"] += 1

    def tick_d(limit):
        n = state["d"]
        if n < limit:
            line_sum.tick(n)
            side_sum.tick(n)
            state["d"] += 1
            state["owed"] = min(state["owed"] + X_PER_D, 2.0)
            while state["owed"] >= 1.0:
                tick_x()
                state["owed"] -= 1.0

    early = gw_out.shape[0] // CHUNK
    middle = early + gw_dense.shape[0] // (2 * CHUNK)

    peers.greet()
    cot_copy = pltpu.make_async_copy(cot_hbm, wide, wide_sem)
    cot_copy.start()
    tick_d(early)
    lane_head = lax.broadcasted_iota(jnp.int32, (1, width), 1) >> 6
    row_head = lax.broadcasted_iota(jnp.int32, (width, 1), 0) >> 6

    def head_lanes(h):
        return (lane_head == h).astype(jnp.float32).astype(jnp.bfloat16)

    def head_rows(h):
        return (row_head == h).astype(jnp.float32).astype(jnp.bfloat16)

    q_t[...] = q[...].T
    k_t[...] = k[...].T
    v_t[...] = v[...].T
    cot_copy.wait()
    for t in range(tiles):
        rows = pl.ds(t * TILE, TILE)
        do[rows] = mm(wide[rows], w_dense[...], NT).astype(jnp.bfloat16)
    do_t[...] = do[...].T

    def load(hbm, buf, sem, t):
        copy = pltpu.make_async_copy(hbm.at[pl.ds(t * TILE, TILE)], buf, sem)
        copy.start()
        return copy

    def send_out(value, part, rows):
        settle()
        stage_out[...] = value
        state["push"] = pltpu.make_async_copy(stage_out, part.at[rows], out_sem)
        state["push"].start()
        state["made"] += 1

    def span(i):
        return min(i + 2, tiles) * TILE

    for i in range(tiles):
        fetch = load(mlp_hbm, stage_in, in_sem, i)
        n, cols = span(i), pl.ds(i * TILE, TILE)

        def head_forward(h, _):
            rows = pl.ds(pl.multiple_of(h * HD, HD), HD)
            q_head = q_t[:, cols] * head_rows(h)
            top = None
            for start in range(0, n, TILE):
                keys = pl.ds(start, TILE)
                tile_scores = mm(k[keys], q_head)
                if start >= i * TILE:
                    allowed = ids_col[keys, :] <= ids_row[:, cols]
                    tile_scores = jnp.where(allowed, tile_scores, -1e30)
                scores[keys] = tile_scores
                tile_top = jnp.max(tile_scores, axis=0, keepdims=True)
                top = tile_top if top is None else jnp.maximum(top, tile_top)
            total = jnp.zeros_like(top)
            for start in range(0, n, TILE):
                keys = pl.ds(start, TILE)
                weights = jnp.exp(scores[keys] - top)
                total += jnp.sum(weights, axis=0, keepdims=True)
                probs[keys, 0:TILE] = weights.astype(jnp.bfloat16)
            head_out = mm(v_t[rows, 0:n], probs[0:n, 0:TILE]) / total
            lse[pl.ds(h, 1), cols] = top + jnp.log(total)
            delta[pl.ds(h, 1), cols] = jnp.sum(
                head_out * do_t[rows, cols].astype(jnp.float32), axis=0, keepdims=True
            )
            dq_t[rows, cols] = head_out
            return 0

        lax.fori_loop(0, heads, head_forward, 0)
        mixed_tile = dq_t[:, cols].T.astype(jnp.bfloat16)
        mixed[cols] = mixed_tile
        fetch.wait()
        send_out(mm(mixed_tile, w_dense[...]) + stage_in[...], out_part, cols)
        tick_d(early)

    def put_grad(value, part, row):
        cols = value.shape[1]
        stage_w[:, 0:cols] = value
        copy = pltpu.make_async_copy(
            stage_w.at[:, pl.ds(0, cols)], part.at[pl.ds(row, value.shape[0])], w_sem
        )
        copy.start()
        copy.wait()

    put_grad(mm(mixed[...], wide[...], TN), gw_dense, 0)
    normed_copy = pltpu.make_async_copy(normed_hbm, wide, wide_sem)
    normed_copy.start()

    def rotate_back(grad):
        halves = []
        for part in range(width // 128):
            g = grad[:, part * 128 : (part + 1) * 128]
            halves.append(
                g * stage_t[0]
                - pltpu.roll(g, 120, 1) * stage_t[1]
                - pltpu.roll(g, 8, 1) * stage_t[2]
            )
        return jnp.concatenate(halves, axis=1)

    def fetches(t):
        table = pltpu.make_async_copy(tables_hbm.at[:, pl.ds(t * TILE, TILE)], stage_t, t_sem)
        table.start()
        return table, load(dn_hbm, stage_in, in_sem, t), load(x_hbm, stage_x, x_sem, t)

    def finish(t, copies):
        rows = pl.ds(t * TILE, TILE)
        for copy in copies:
            copy.wait()
        dq_tile = rotate_back(dq_t[:, rows].T * (HD**-0.5))
        dk_tile = rotate_back(dk[rows])
        joined = jnp.concatenate([dq_tile, dk_tile, dv[rows]], axis=1).astype(jnp.bfloat16)
        laid = mm(joined, perm[...])
        dproj[rows] = laid.astype(jnp.bfloat16)
        rows_sum[4:5, 0 : 3 * width] += jnp.sum(laid, axis=0, keepdims=True)
        d_tile = mm(dproj[rows], w_qkv[...], NT) + stage_in[...]
        send_out(d_tile, dnorm_part, rows)
        centred = stage_x[...].astype(jnp.float32)
        centred = centred - jnp.mean(centred, axis=1, keepdims=True)
        spread = jnp.mean(centred * centred, axis=1, keepdims=True)
        standard = centred * lax.rsqrt(spread + eps)
        rows_sum[0:1] += jnp.sum(d_tile * standard, axis=0, keepdims=True)
        rows_sum[1:2] += jnp.sum(d_tile, axis=0, keepdims=True)

    rows_sum[...] = small[...]
    for i in reversed(range(tiles)):
        n, cols = span(i), pl.ds(i * TILE, TILE)
        copies = fetches(i + 1) if i < tiles - 1 else None
        for h in range(heads):
            stack_a[h * TILE : (h + 1) * TILE] = do[cols] * head_lanes(h)
            stack_b[h * TILE : (h + 1) * TILE] = q[cols] * head_lanes(h)

        def head_backward(h, _):
            rows = pl.ds(pl.multiple_of(h * HD, HD), HD)
            block = pl.ds(pl.multiple_of(h * TILE, TILE), TILE)
            q_head, do_head = q_t[:, cols] * head_rows(h), do_t[:, cols] * head_rows(h)
            shift, row_delta = lse[pl.ds(h, 1), cols], delta[pl.ds(h, 1), cols]
            for start in range(0, n, TILE):
                keys = pl.ds(start, TILE)
                tile_scores = mm(k[keys], q_head)
                if start >= i * TILE:
                    allowed = ids_col[keys, :] <= ids_row[:, cols]
                    tile_scores = jnp.where(allowed, tile_scores, -1e30)
                weights = jnp.exp(tile_scores - shift)
                probs[keys, block] = weights.astype(jnp.bfloat16)
                d_tile = weights * (mm(v[keys], do_head) - row_delta)
                dscores[keys, block] = d_tile.astype(jnp.bfloat16)
            dq_t[rows, cols] = mm(k_t[rows, 0:n], dscores[0:n, block])
            return 0

        lax.fori_loop(0, heads, head_backward, 0)
        tick_d(middle)
        for grad, left, right in ((dv, probs, stack_a), (dk, dscores, stack_b)):
            for start in range(0, n, 2 * TILE):
                keys = pl.ds(start, min(2 * TILE, n - start))
                term = mm(left[keys], right[...])
                grad[keys] = term if i == tiles - 1 else grad[keys] + term
        if i < tiles - 1:
            finish(i + 1, copies)
    finish(0, fetches(0))
    little.start(rows_sum[...])
    normed_copy.wait()
    for row in range(0, d, TILE):
        put_grad(mm(wide[:, row : row + TILE], dproj[...], TN), gw_qkv, row)
    for t in range(max(len(line), len(side)) + STAGES - 1):
        tick_d(max(len(line), len(side)) + STAGES - 1)
        if t < 5:
            little.step(t)
    small_sum[0:8] = little.kept[3]
    small_sum[8:16] = little.kept[5]
    for t in range(len(tensor_sum.chunks) + 3):
        tick_x()


X_PER_D = 0.67


def attention(dp_size, q, k, v, ids, cot, normed, w_dense, w_qkv, tables, x, mlp, dn, gw_out, gw_in, small):
    tokens, width = q.shape
    heads = width // HD
    d = x.shape[1]
    c = 3 * width
    order = np.arange(c).reshape(3, heads, HD).transpose(1, 0, 2).reshape(-1)
    perm = np.zeros((c, c), np.float32)
    perm[order, np.arange(c)] = 1.0
    vm = pl.BlockSpec(memory_space=pltpu.VMEM)
    hbm = pl.BlockSpec(memory_space=pl.ANY)
    f32, bf16 = jnp.float32, jnp.bfloat16
    dma = pltpu.SemaphoreType.DMA
    scratch = [
        pltpu.VMEM((width, tokens), bf16),
        pltpu.VMEM((width, tokens), bf16),
        pltpu.VMEM((width, tokens), bf16),
        pltpu.VMEM((tokens, width), bf16),
        pltpu.VMEM((width, tokens), bf16),
        pltpu.VMEM((tokens, TILE), f32),
        pltpu.VMEM((tokens, heads * TILE), bf16),
        pltpu.VMEM((tokens, heads * TILE), bf16),
        pltpu.VMEM((heads * TILE, width), bf16),
        pltpu.VMEM((heads * TILE, width), bf16),
        pltpu.VMEM((tokens, width), f32),
        pltpu.VMEM((tokens, width), f32),
        pltpu.VMEM((width, tokens), f32),
        pltpu.VMEM((tokens, width), bf16),
        pltpu.VMEM((8, tokens), f32),
        pltpu.VMEM((8, tokens), f32),
        pltpu.VMEM((tokens, c), bf16),
        pltpu.VMEM((tokens, d), bf16),
        pltpu.VMEM((8, d), f32),
        pltpu.VMEM((TILE, d), f32),
        pltpu.VMEM((TILE, d), bf16),
        pltpu.VMEM((3, TILE, 128), f32),
        pltpu.VMEM((TILE, d), f32),
        pltpu.VMEM((TILE, d), f32),
        dma,
        dma,
        dma,
        dma,
        dma,
        dma,
    ]
    scratch += LineFirst.scratch() + SideFirst.scratch() + SmallSum.scratch() + TensorSum.scratch()

    def shape(*dims):
        return jax.ShapeDtypeStruct(dims, f32)

    outs = pl.pallas_call(
        functools.partial(attention_kernel, heads, dp_size),
        out_shape=(
            shape(tokens, d),
            shape(tokens, d),
            shape(*gw_out.shape),
            shape(*gw_in.shape),
            shape(width, d),
            shape(d, c),
            shape(16, d),
            shape(tokens, d),
            shape(tokens, d),
            shape(width, d),
            shape(d, c),
        ),
        in_specs=[vm] * 9 + [hbm] * 8,
        out_specs=(hbm,) * 6 + (vm,) + (hbm,) * 4,
        scratch_shapes=scratch,
        compiler_params=pltpu.CompilerParams(
            collective_id=0, has_side_effects=True, vmem_limit_bytes=61 << 20
        ),
        name="attention",
    )(
        q,
        k,
        v,
        ids[:, None],
        ids[None, :],
        w_dense,
        w_qkv,
        jnp.asarray(perm, bf16),
        small,
        cot,
        normed,
        tables,
        x,
        mlp,
        dn,
        gw_out,
        gw_in,
    )
    return outs[:7]


SLOTS = 5
STAGES = 6
CHUNK = 64
MESH_ID = pl.DeviceIdType.MESH


def z_stride(group):
    return 2 if group == 8 else 4


class Peers:
    def __init__(self, dp_size):
        stride = z_stride(dp_size)
        d, t = lax.axis_index("dp"), lax.axis_index("tensor")
        z = lax.rem(lax.div(d, stride), 4)
        base = d - z * stride
        self.y_half = lax.rem(d, 2)
        self.z_half = lax.div(z, 2)
        self.middle = jnp.logical_or(z == 1, z == 2)
        self.end = jnp.logical_or(z == 0, z == 3)
        self.y = (d + 1 - 2 * self.y_half, t)
        self.z_pair = (base + stride * (z + 1 - 2 * lax.rem(z, 2)), t)
        self.z_mid = (base + stride * (3 - z), t)
        self.z_far = (base + stride * lax.rem(z + 2, 4), t)
        self.core_half = lax.rem(t, 2)
        self.core = (d, t + 1 - 2 * lax.rem(t, 2))
        self.x = (d, lax.rem(t + 2, 4))

    def greet(self):
        barrier = pltpu.get_barrier_semaphore()
        partners = (self.y, self.z_pair, self.z_mid, self.z_far, self.core, self.x)
        for partner in partners:
            pl.semaphore_signal(barrier, inc=1, device_id=partner, device_id_type=MESH_ID)
        pl.semaphore_wait(barrier, len(partners))


def remote(src, dst, sems, index, device):
    return pltpu.make_async_remote_copy(
        src_ref=src,
        dst_ref=dst,
        send_sem=sems.at[(0,) + index],
        recv_sem=sems.at[(1,) + index],
        device_id=device,
        device_id_type=MESH_ID,
    )


class LineFirst:
    def __init__(self, peers, chunks, scratch):
        self.p, self.chunks = peers, chunks
        self.land, self.work, self.mid, self.side, self.done, self.sems, self.local = scratch

    @staticmethod
    def scratch():
        f32 = jnp.float32
        return [
            pltpu.VMEM((SLOTS, CHUNK, 1024), f32),
            pltpu.VMEM((SLOTS, CHUNK, 1024), f32),
            pltpu.VMEM((SLOTS, CHUNK // 2, 1024), f32),
            pltpu.VMEM((SLOTS, CHUNK // 2, 1024), f32),
            pltpu.VMEM((SLOTS, CHUNK, 1024), f32),
            pltpu.SemaphoreType.DMA((2, 5, SLOTS)),
            pltpu.SemaphoreType.DMA((2, SLOTS)),
        ]

    def stage(self, c, s):
        p, slot = self.p, c % SLOTS
        part, total, row, cols = self.chunks[c]
        rows, lanes = pl.ds(row, CHUNK), pl.ds(0, cols)
        half = CHUNK // 2
        own = pl.ds(pl.multiple_of(p.z_half * half, half), half)
        other = pl.ds(pl.multiple_of((1 - p.z_half) * half, half), half)
        land, work = self.land.at[slot, :, lanes], self.work.at[slot, :, lanes]
        mid, side = self.mid.at[slot, :, lanes], self.side.at[slot, :, lanes]
        done = self.done.at[slot, :, lanes]
        inward = functools.partial(remote, part.at[rows], land, self.sems, (0, slot), p.z_pair)
        across = functools.partial(remote, work.at[other], mid, self.sems, (1, slot), p.z_mid)
        beside = functools.partial(remote, work.at[own], side, self.sems, (2, slot), p.y)
        back = functools.partial(remote, done.at[own], done.at[own], self.sems, (3, slot), p.z_mid)
        outward = functools.partial(remote, done, total.at[rows], self.sems, (4, slot), p.z_pair)
        fetch = functools.partial(pltpu.make_async_copy, part.at[rows], work, self.local.at[0, slot])
        store = functools.partial(pltpu.make_async_copy, done, total.at[rows], self.local.at[1, slot])

        if s == 0:

            @pl.when(p.end)
            def _():
                inward().start()

            @pl.when(p.middle)
            def _():
                fetch().start()

        if s == 5:

            @pl.when(p.end)
            def _():
                outward().wait_recv()
                inward().wait_send()

        if s > 0:

            @pl.when(p.middle)
            def _():
                if s == 1:
                    fetch().wait()
                    inward().wait_recv()
                    work[...] += land[...]
                    across().start()
                if s == 2:
                    across().wait_recv()
                    work[own] += mid[...]
                    beside().start()
                if s == 3:
                    beside().wait_recv()
                    done[own] = work[own] + side[...]
                    back().start()
                if s == 4:
                    back().wait_recv()
                    outward().start()
                    store().start()
                if s == 5:
                    for copy in (across, beside, back, outward):
                        copy().wait_send()
                    store().wait()

    def tick(self, t):
        for s in reversed(range(STAGES)):
            if 0 <= t - s < len(self.chunks):
                self.stage(t - s, s)


class SideFirst:
    def __init__(self, peers, chunks, scratch):
        self.p, self.chunks = peers, chunks
        self.land, self.work, self.line, self.mid, self.done, self.sems, self.local = scratch

    @staticmethod
    def scratch():
        return [pltpu.VMEM((SLOTS, CHUNK // 2, 1024), jnp.float32)] * 5 + [
            pltpu.SemaphoreType.DMA((2, 5, SLOTS)),
            pltpu.SemaphoreType.DMA((2, SLOTS)),
        ]

    def stage(self, c, s):
        p, slot = self.p, c % SLOTS
        part, total, row, cols = self.chunks[c]
        lanes, half = pl.ds(0, cols), CHUNK // 2
        own = pl.ds(pl.multiple_of(row + p.y_half * half, half), half)
        other = pl.ds(pl.multiple_of(row + (1 - p.y_half) * half, half), half)
        land, work = self.land.at[slot, :, lanes], self.work.at[slot, :, lanes]
        line, mid = self.line.at[slot, :, lanes], self.mid.at[slot, :, lanes]
        done = self.done.at[slot, :, lanes]
        beside = functools.partial(remote, part.at[other], land, self.sems, (0, slot), p.y)
        inward = functools.partial(remote, work, line, self.sems, (1, slot), p.z_pair)
        across = functools.partial(remote, work, mid, self.sems, (2, slot), p.z_mid)
        outward = functools.partial(remote, done, done, self.sems, (3, slot), p.z_pair)
        back = functools.partial(remote, done, total.at[own], self.sems, (4, slot), p.y)
        fetch = functools.partial(pltpu.make_async_copy, part.at[own], work, self.local.at[0, slot])
        store = functools.partial(pltpu.make_async_copy, done, total.at[own], self.local.at[1, slot])

        if s == 0:
            beside().start()
            fetch().start()
        if s == 1:
            fetch().wait()
            beside().wait_recv()
            work[...] += land[...]

            @pl.when(p.end)
            def _():
                inward().start()

        if s in (2, 3):

            @pl.when(p.middle)
            def _():
                if s == 2:
                    inward().wait_recv()
                    work[...] += line[...]
                    across().start()
                if s == 3:
                    across().wait_recv()
                    done[...] = work[...] + mid[...]
                    outward().start()

        if s == 4:

            @pl.when(p.end)
            def _():
                outward().wait_recv()

            back().start()
            store().start()
        if s == 5:
            back().wait()
            beside().wait_send()
            store().wait()

            @pl.when(p.end)
            def _():
                inward().wait_send()

            @pl.when(p.middle)
            def _():
                across().wait_send()
                outward().wait_send()

    def tick(self, t):
        for s in reversed(range(STAGES)):
            if 0 <= t - s < len(self.chunks):
                self.stage(t - s, s)


class SmallSum:
    def __init__(self, peers, scratch):
        self.p = peers
        self.kept, self.got, self.sems = scratch

    @staticmethod
    def scratch():
        return [
            pltpu.VMEM((6, 8, 1024), jnp.float32),
            pltpu.VMEM((5, 8, 1024), jnp.float32),
            pltpu.SemaphoreType.DMA((2, 5)),
        ]

    def copy(self, s):
        p = self.p
        partner = (p.y, p.z_pair, p.z_far, p.core, p.x)[s]
        return remote(self.kept.at[s], self.got.at[s], self.sems, (s,), partner)

    def start(self, rows):
        self.kept[0] = rows
        self.copy(0).start()

    def step(self, s):
        self.copy(s).wait()
        self.kept[s + 1] = self.kept[s] + self.got[s]
        if s < 4:
            self.copy(s + 1).start()


class TensorSum:
    def __init__(self, peers, chunks, scratch):
        self.p, self.chunks = peers, chunks
        self.land, self.work, self.mid, self.done, self.sems, self.local = scratch

    @staticmethod
    def scratch():
        return [pltpu.VMEM((3, TILE // 2, 1024), jnp.float32)] * 4 + [
            pltpu.SemaphoreType.DMA((2, 3, 3)),
            pltpu.SemaphoreType.DMA((2, 3)),
        ]

    def stage(self, c, s):
        p, slot, half = self.p, c % 3, TILE // 2
        part, total, row = self.chunks[c]
        own = pl.ds(pl.multiple_of(row + p.core_half * half, half), half)
        other = pl.ds(pl.multiple_of(row + (1 - p.core_half) * half, half), half)
        land, work, mid, done = (r.at[slot] for r in (self.land, self.work, self.mid, self.done))
        beside = functools.partial(remote, part.at[other], land, self.sems, (0, slot), p.core)
        across = functools.partial(remote, work, mid, self.sems, (1, slot), p.x)
        back = functools.partial(remote, done, total.at[own], self.sems, (2, slot), p.core)
        fetch = functools.partial(pltpu.make_async_copy, part.at[own], work, self.local.at[0, slot])
        store = functools.partial(pltpu.make_async_copy, done, total.at[own], self.local.at[1, slot])
        if s == 0:
            beside().start()
            fetch().start()
        if s == 1:
            fetch().wait()
            beside().wait_recv()
            work[...] += land[...]
            across().start()
        if s == 2:
            across().wait_recv()
            done[...] = work[...] + mid[...]
            back().start()
            store().start()
        if s == 3:
            beside().wait_send()
            across().wait_send()
            back().wait()
            store().wait()

    def tick(self, t):
        for s in reversed(range(4)):
            if 0 <= t - s < len(self.chunks):
                self.stage(t - s, s)


def chunk_lists(parts, totals):
    ways = ([], [])
    for turn, (part, total) in enumerate(zip(parts, totals)):
        for i in range(part.shape[0] // CHUNK):
            ways[(turn if turn < 2 else i) % 2].append((part, total, i * CHUNK, part.shape[1]))
    return ways


def rest_groups(dp_size):
    stride = z_stride(dp_size)
    places = np.arange(dp_size).reshape(-1, 4, stride // 2, 2)
    return places.transpose(1, 3, 0, 2).reshape(8, -1).tolist()


def rotate(source, tables):
    tokens, width = source.shape
    cos_t, low_t, high_t = tables
    pairs = source.reshape(tokens, width // 128, 128)
    up = jnp.roll(pairs, -8, axis=2)
    down = jnp.roll(pairs, 8, axis=2)
    turned = pairs * cos_t[:, None] + up * low_t[:, None] + down * high_t[:, None]
    return turned.reshape(tokens, width)


def norm_back(d_rows, std_rows, inv_rows, cot_rows, gain):
    scaled = d_rows * gain
    inner = (
        scaled
        - jnp.mean(scaled, axis=-1, keepdims=True)
        - std_rows * jnp.mean(scaled * std_rows, axis=-1, keepdims=True)
    )
    return cot_rows + inv_rows * inner


def on_device(
    dp_size,
    layer_input,
    positions,
    block_ids,
    ln_gain,
    ln_bias,
    w_qkv,
    b_qkv,
    w_dense,
    b_dense,
    w_in,
    b_in,
    w_out,
    b_out,
    cotangent,
):
    d = layer_input.shape[1]
    width = w_dense.shape[0]
    heads = width // HD
    input_float = layer_input.astype(jnp.float32)
    row_mean = jnp.mean(input_float, axis=-1, keepdims=True)
    centred = input_float - row_mean
    variance = jnp.mean(centred * centred, axis=-1, keepdims=True)
    inv_std = lax.rsqrt(variance + eps)
    standard = centred * inv_std
    normed = (standard * ln_gain + ln_bias).astype(jnp.bfloat16)
    tables = lane_tables(positions)
    w_parts = w_qkv.reshape(d, heads, 3, HD).transpose(2, 0, 1, 3).reshape(3, d, width)
    b_parts = b_qkv.reshape(heads, 3, HD).transpose(1, 0, 2).reshape(3, width)

    def project(part):
        return jnp.dot(normed, w_parts[part], preferred_element_type=jnp.float32) + b_parts[part]

    query = rotate(project(0), tables).astype(jnp.bfloat16) * jnp.bfloat16(HD**-0.5)
    keys = rotate(project(1), tables).astype(jnp.bfloat16)
    values = project(2).astype(jnp.bfloat16)

    hidden = jnp.dot(normed, w_in, preferred_element_type=jnp.float32) + b_in
    normal_cdf = 0.5 * (1.0 + lax.erf(hidden * 0.7071067811865476))
    activated = (hidden * normal_cdf).astype(jnp.bfloat16)
    mlp_part = jnp.dot(activated, w_out, preferred_element_type=jnp.float32)
    cot_float = cotangent.astype(jnp.float32)
    bias_grad = jnp.sum(cot_float, axis=0)
    grad_w_out = jnp.einsum("tf,td->fd", activated, cotangent, preferred_element_type=jnp.float32)
    d_activated = jnp.dot(cotangent, w_out.T, preferred_element_type=jnp.float32)
    normal_pdf = jnp.exp(-0.5 * hidden * hidden) * 0.3989422804014327
    d_hidden = (d_activated * (normal_cdf + hidden * normal_pdf)).astype(jnp.bfloat16)
    grad_w_in = jnp.einsum("td,tf->df", normed, d_hidden, preferred_element_type=jnp.float32)
    grad_b_in = jnp.sum(d_hidden, axis=0, dtype=jnp.float32)
    d_mlp = jnp.dot(d_hidden, w_in.T, preferred_element_type=jnp.float32)

    zero = jnp.zeros((d,), jnp.float32)
    small = jnp.stack([zero, zero, bias_grad, grad_b_in] + [zero] * 4)
    branches, d_full, *sums = attention(
        dp_size,
        query,
        keys,
        values,
        block_ids,
        cotangent,
        normed,
        w_dense,
        w_qkv,
        jnp.stack(tables),
        layer_input,
        mlp_part,
        d_mlp,
        grad_w_out,
        grad_w_in,
        small,
    )
    if dp_size > 8:
        sums = lax.psum(sums, "dp", axis_index_groups=rest_groups(dp_size))
    grad_w_out, grad_w_in, grad_w_dense, grad_w_qkv, small = sums
    bias_grad, grad_b_in, grad_b_qkv = small[2], small[3], small[4, : 3 * width]
    grad_gain, grad_shift = small[8], small[9]
    output = (input_float + branches + b_dense + b_out).astype(jnp.bfloat16)
    grad_input = norm_back(d_full, standard, inv_std, cot_float, ln_gain)
    return (
        output,
        grad_input,
        grad_gain,
        grad_shift,
        grad_w_qkv,
        grad_b_qkv,
        grad_w_dense,
        bias_grad,
        grad_w_in,
        grad_b_in,
        grad_w_out,
        bias_grad,
    )


def solution(mesh):
    in_specs = (
        P("dp", None),
        P("dp"),
        P("dp"),
        P(),
        P(),
        P(None, "tensor"),
        P("tensor"),
        P("tensor", None),
        P(),
        P(None, "tensor"),
        P("tensor"),
        P("tensor", None),
        P(),
        P("dp", None),
    )
    out_specs = (
        P("dp", None),
        P("dp", None),
        P(),
        P(),
        P(None, "tensor"),
        P("tensor"),
        P("tensor", None),
        P(),
        P(None, "tensor"),
        P("tensor"),
        P("tensor", None),
        P(),
    )
    return jax.shard_map(
        functools.partial(on_device, mesh.shape["dp"]), mesh=mesh, in_specs=in_specs, out_specs=out_specs, check_vma=False
    )
```

```python
import functools

import jax
import jax.numpy as jnp
import numpy as np
from jax import lax
from jax.experimental import pallas as pl
from jax.experimental.pallas import tpu as pltpu
from jax.sharding import PartitionSpec as P

HD = 64
ROT = 16
TILE = 256

eps = 1e-05
rotary_base = 10000.0
NT = (((1,), (1,)), ((), ()))
TN = (((0,), (0,)), ((), ()))
NN = (((1,), (0,)), ((), ()))


def mm(a, b, dims=NN):
    return lax.dot_general(a, b, dims, preferred_element_type=jnp.float32)


def layer_kernel(
    heads,
    dp_size,
    ids_row,
    trig,
    vecs,
    w_dense,
    x_hbm,
    cot_hbm,
    w_qkv_hbm,
    w_in_hbm,
    w_out_hbm,
    output,
    grad_input,
    sum_w_out,
    sum_w_in,
    sum_w_dense,
    sum_w_qkv,
    small_sum,
    out_part,
    dnorm_part,
    gw_out,
    gw_in,
    gw_dense,
    gw_qkv,
    act_hbm,
    dh_hbm,
    normed_hbm,
    q,
    k,
    v,
    q_t,
    k_t,
    v_t,
    do,
    do_t,
    scores,
    probs,
    dscores,
    stack_a,
    stack_b,
    dk,
    dv,
    dq_t,
    mixed,
    lse,
    delta,
    ids_col,
    w_in,
    w_out,
    w_cols,
    rows_sum,
    stage_h,
    stage_x,
    stage_out,
    stage_w,
    big_sem,
    h_sem,
    x_sem,
    out_sem,
    w_sem,
    spill_sem,
    *comm,
):
    tokens, d = x_hbm.shape
    tiles = tokens // TILE
    width = heads * HD
    ff = w_out.shape[0]
    f32, bf16 = jnp.float32, jnp.bfloat16
    parts = len(LineFirst.scratch())
    peers = Peers(dp_size)
    line, side = chunk_lists(
        (gw_out, gw_in, gw_dense, gw_qkv), (sum_w_out, sum_w_in, sum_w_dense, sum_w_qkv)
    )
    line_sum = LineFirst(peers, line, comm[:parts])
    side_sum = SideFirst(peers, side, comm[parts : 2 * parts])
    little = SmallSum(peers, comm[2 * parts : 2 * parts + 3])
    tensor_sum = TensorSum(
        peers,
        [(out_part, t * TILE, False) for t in range(tiles)]
        + [(dnorm_part, t * TILE, True) for t in reversed(range(tiles))],
        (x_hbm, cot_hbm, vecs, output, grad_input),
        comm[2 * parts + 3 :],
    )
    rounds = max(len(line), len(side)) + STAGES - 1
    state = {"d": 0, "x": 0, "made": 0, "push": None, "ready": 0, "due_d": 0.0, "due_x": 0.0}

    def settle():
        if state["push"] is not None:
            state["push"].wait()
            state["push"] = None

    def tick_x():
        n, last = state["x"], len(tensor_sum.chunks)
        if n < min(state["made"], last) or (state["made"] == last and n < last + X_DELAYS[-1]):
            settle()
            tensor_sum.tick(n)
            state["x"] += 1
            return True
        return False

    def tick_d():
        n = state["d"]
        if n < (state["ready"] if state["ready"] < len(line) else rounds):
            line_sum.tick(n)
            side_sum.tick(n)
            state["d"] += 1
            return True
        return False

    def worked(us):
        for way, pace, step in (("due_d", D_PACE, tick_d), ("due_x", X_PACE, tick_x)):
            state[way] = min(state[way] + us, 2 * pace)
            if state[way] >= pace and step():
                state[way] -= pace

    def begin(src, dst, sem):
        copy = pltpu.make_async_copy(src, dst, sem)
        copy.start()
        return copy

    def tile_rows(t):
        return pl.ds(t * TILE, TILE)

    lane_head = lax.broadcasted_iota(jnp.int32, (1, width), 1) >> 6
    row_head = lax.broadcasted_iota(jnp.int32, (width, 1), 0) >> 6

    def head_lanes(h):
        return (lane_head == h).astype(f32).astype(bf16)

    def head_rows(h):
        return (row_head == h).astype(f32).astype(bf16)

    peers.greet()
    qkv_copy = begin(w_qkv_hbm, w_in.at[:, pl.ds(0, 3 * width)], big_sem.at[0])
    x_copy = begin(x_hbm.at[tile_rows(0)], stage_x.at[0], x_sem.at[0])
    cot_copy = begin(cot_hbm, dscores, big_sem.at[1])
    w_out_copy = begin(w_out_hbm, w_out, big_sem.at[2])
    qkv_copy.wait()
    for part in range(3):
        pieces = [w_in[:, (3 * h + part) * HD : (3 * h + part + 1) * HD] for h in range(heads)]
        w_cols[:, part * width : (part + 1) * width] = jnp.concatenate(pieces, axis=1)
    w_in_copy = begin(w_in_hbm, w_in, big_sem.at[0])

    normed = probs
    gain, shift = vecs[0:1], vecs[1:2]
    for t in range(tiles):
        x_copy.wait()
        if t + 1 < tiles:
            slot = (t + 1) % 2
            next_copy = begin(x_hbm.at[tile_rows(t + 1)], stage_x.at[slot], x_sem.at[slot])
        standard, _ = standardize(stage_x[t % 2])
        normed[tile_rows(t)] = (standard * gain + shift).astype(bf16)
        x_copy = next_copy
        ids_tile = jnp.broadcast_to(ids_row[:, t * TILE : (t + 1) * TILE], (8, TILE))
        ids_col[tile_rows(t)] = ids_tile.T
    normed_copy = begin(normed, normed_hbm, spill_sem.at[0])

    act_block, dh_block = mixed, do
    rows_sum[...] = jnp.zeros_like(rows_sum)
    cot_copy.wait()
    w_in_copy.wait()
    w_out_copy.wait()
    spills, puts = [], []

    def put_grad(value, part, row, slot):
        stage_w[slot] = value
        return begin(stage_w.at[slot], part.at[pl.ds(row, TILE)], w_sem.at[slot])

    for c in range(ff // TILE):
        units = pl.ds(c * TILE, TILE)
        for copy in spills:
            copy.wait()
        for start in range(0, tokens, 2 * TILE):
            rows = pl.ds(start, 2 * TILE)
            hidden = mm(normed[rows], w_in[:, units]) + vecs[2:3, units]
            normal_cdf = 0.5 * (1.0 + lax.erf(hidden * 0.7071067811865476))
            act_block[rows] = (hidden * normal_cdf).astype(bf16)
            normal_pdf = jnp.exp(-0.5 * hidden * hidden) * 0.3989422804014327
            d_active = mm(dscores[rows], w_out[units], NT)
            d_hidden = (d_active * (normal_cdf + hidden * normal_pdf)).astype(bf16)
            dh_block[rows] = d_hidden
            rows_sum[3:4, units] += jnp.sum(d_hidden.astype(f32), axis=0, keepdims=True)
        spills = [
            begin(act_block, act_hbm.at[:, units], spill_sem.at[1]),
            begin(dh_block, dh_hbm.at[:, units], spill_sem.at[2]),
        ]
        worked(3.6)
        puts = [
            put_grad(mm(act_block[...], dscores[...], TN), gw_out, c * TILE, 0),
            put_grad(mm(dh_block[...], normed[...], TN), gw_in, c * TILE, 1),
        ]
        for copy in puts:
            copy.wait()
        state["ready"] += TILE // CHUNK
        worked(2.4)
    for copy in spills:
        copy.wait()

    half = ROT // 2
    still = jnp.ones((HD - ROT, TILE), f32)
    none = jnp.zeros((HD - ROT, TILE), f32)
    blank = jnp.zeros((half, TILE), f32)

    def lane_tables(cols):
        cosine, sine = trig[0:half, cols], trig[half : 2 * half, cols]
        cos_head = [cosine, cosine, still]
        low_head = [-sine, blank, none]
        high_head = [blank, sine, none]
        return tuple(jnp.concatenate(t + t, axis=0).T for t in (cos_head, low_head, high_head))

    def turn(value, tables, sign):
        cos_t, low_t, high_t = tables
        halves = []
        for part in range(width // 128):
            g = value[:, part * 128 : (part + 1) * 128]
            moved = pltpu.roll(g, 120, 1) * low_t + pltpu.roll(g, 8, 1) * high_t
            halves.append(g * cos_t + sign * moved)
        return jnp.concatenate(halves, axis=1)

    for t in range(tiles):
        rows = tile_rows(t)
        tables = lane_tables(rows)
        projected = mm(normed[rows], w_cols[...]) + vecs[5:6, 0 : 3 * width]
        query = turn(projected[:, 0:width], tables, 1.0).astype(bf16) * HD**-0.5
        key = turn(projected[:, width : 2 * width], tables, 1.0).astype(bf16)
        value = projected[:, 2 * width :].astype(bf16)
        d_out = mm(dscores[rows], w_dense[...], NT).astype(bf16)
        q[rows], k[rows], v[rows], do[rows] = query, key, value, d_out
        q_t[:, rows], k_t[:, rows], v_t[:, rows], do_t[:, rows] = query.T, key.T, value.T, d_out.T
        rows_sum[2:3] += jnp.sum(dscores[rows].astype(f32), axis=0, keepdims=True)
        worked(0.7)
    normed_copy.wait()

    def send_out(value, part, rows):
        settle()
        stage_out[...] = value
        state["push"] = begin(stage_out, part.at[rows], out_sem)
        state["made"] += 1

    def span(i):
        return min(i + 2, tiles) * TILE

    for i in range(tiles):
        n, cols = span(i), tile_rows(i)
        fetch = begin(act_hbm.at[cols], stage_h, h_sem)

        def head_forward(h, _):
            rows = pl.ds(pl.multiple_of(h * HD, HD), HD)
            q_head = q_t[:, cols] * head_rows(h)
            top = None
            for start in range(0, n, TILE):
                keys = pl.ds(start, TILE)
                tile_scores = mm(k[keys], q_head)
                if start >= i * TILE:
                    allowed = ids_col[keys, 0:1] <= ids_row[:, cols]
                    tile_scores = jnp.where(allowed, tile_scores, -1e30)
                scores[keys] = tile_scores
                tile_top = jnp.max(tile_scores, axis=0, keepdims=True)
                top = tile_top if top is None else jnp.maximum(top, tile_top)
            total = jnp.zeros_like(top)
            for start in range(0, n, TILE):
                keys = pl.ds(start, TILE)
                weights = jnp.exp(scores[keys] - top)
                total += jnp.sum(weights, axis=0, keepdims=True)
                probs[keys, 0:TILE] = weights.astype(bf16)
            head_out = mm(v_t[rows, 0:n], probs[0:n, 0:TILE]) / total
            lse[pl.ds(h, 1), cols] = top + jnp.log(total)
            delta[pl.ds(h, 1), cols] = jnp.sum(
                head_out * do_t[rows, cols].astype(f32), axis=0, keepdims=True
            )
            dq_t[rows, cols] = head_out
            return 0

        lax.fori_loop(0, heads, head_forward, 0)
        mixed_tile = dq_t[:, cols].T.astype(bf16)
        mixed[cols] = mixed_tile
        fetch.wait()
        send_out(mm(mixed_tile, w_dense[...]) + mm(stage_h[...], w_out[...]), out_part, cols)
        worked(1.1 * n / TILE + 0.6)

    put_grad(mm(mixed[...], dscores[...], TN), gw_dense, 0, 0).wait()
    state["ready"] += width // (2 * CHUNK)
    worked(0.8)

    def finish(t, copies):
        rows = tile_rows(t)
        tables = lane_tables(rows)
        for copy in copies:
            copy.wait()
        dq_tile = turn(dq_t[:, rows].T * (HD**-0.5), tables, -1.0).astype(bf16)
        dk_tile = turn(dk[rows], tables, -1.0).astype(bf16)
        dv_tile = dv[rows].astype(bf16)
        q[rows], k[rows], v[rows] = dq_tile, dk_tile, dv_tile
        d_tile = mm(stage_h[...], w_in[...], NT)
        for part, piece in enumerate((dq_tile, dk_tile, dv_tile)):
            lanes = slice(part * width, (part + 1) * width)
            rows_sum[4:5, lanes] += jnp.sum(piece.astype(f32), axis=0, keepdims=True)
            d_tile += mm(piece, w_cols[:, lanes], NT)
        send_out(d_tile, dnorm_part, rows)
        standard, _ = standardize(stage_x[0])
        rows_sum[0:1] += jnp.sum(d_tile * standard, axis=0, keepdims=True)
        rows_sum[1:2] += jnp.sum(d_tile, axis=0, keepdims=True)

    def fetches(t):
        rows = tile_rows(t)
        return (
            begin(dh_hbm.at[rows], stage_h, h_sem),
            begin(x_hbm.at[rows], stage_x.at[0], x_sem.at[0]),
        )

    for i in reversed(range(tiles)):
        n, cols = span(i), tile_rows(i)
        copies = fetches(i + 1) if i < tiles - 1 else None
        for h in range(heads):
            stack_a[h * TILE : (h + 1) * TILE] = do[cols] * head_lanes(h)
            stack_b[h * TILE : (h + 1) * TILE] = q[cols] * head_lanes(h)

        def head_backward(h, _):
            rows = pl.ds(pl.multiple_of(h * HD, HD), HD)
            block = pl.ds(pl.multiple_of(h * TILE, TILE), TILE)
            q_head, do_head = q_t[:, cols] * head_rows(h), do_t[:, cols] * head_rows(h)
            top, row_delta = lse[pl.ds(h, 1), cols], delta[pl.ds(h, 1), cols]
            for start in range(0, n, TILE):
                keys = pl.ds(start, TILE)
                tile_scores = mm(k[keys], q_head)
                if start >= i * TILE:
                    allowed = ids_col[keys, 0:1] <= ids_row[:, cols]
                    tile_scores = jnp.where(allowed, tile_scores, -1e30)
                weights = jnp.exp(tile_scores - top)
                probs[keys, block] = weights.astype(bf16)
                d_tile = weights * (mm(v[keys], do_head) - row_delta)
                dscores[keys, block] = d_tile.astype(bf16)
            dq_t[rows, cols] = mm(k_t[rows, 0:n], dscores[0:n, block])
            return 0

        lax.fori_loop(0, heads, head_backward, 0)
        worked(0.9 * n / TILE)
        for grad, left, right in ((dv, probs, stack_a), (dk, dscores, stack_b)):
            for start in range(0, n, 2 * TILE):
                keys = pl.ds(start, min(2 * TILE, n - start))
                term = mm(left[keys], right[...])
                grad[keys] = term if i == tiles - 1 else grad[keys] + term
        if i < tiles - 1:
            finish(i + 1, copies)
        worked(0.3 * n / TILE + 1.0)
    normed_copy = begin(normed_hbm, probs, spill_sem.at[0])
    finish(0, fetches(0))
    little.start(rows_sum[...])
    normed_copy.wait()
    for part, piece in enumerate((q, k, v)):
        put_grad(mm(piece[...], probs[...], TN), gw_qkv, part * width, 0).wait()
        state["ready"] += width // (2 * CHUNK)
        worked(0.8)

    for s in range(5):
        worked(D_PACE)
        little.step(s)
    small_sum[0:8] = little.kept[3]
    small_sum[8:16] = little.kept[5]
    while state["d"] < rounds:
        worked(D_PACE)
    while tick_x():
        pass
    tensor_sum.settle()


D_PACE = 7.6
X_PACE = 11.4
X_DELAYS = (0, 1, 3, 4)


def standardize(rows):
    centred = rows.astype(jnp.float32)
    centred = centred - jnp.mean(centred, axis=1, keepdims=True)
    inv_std = lax.rsqrt(jnp.mean(centred * centred, axis=1, keepdims=True) + eps)
    return centred * inv_std, inv_std


def layer_call(dp_size, ids_row, trig, vecs, w_dense, x, cot, w_qkv, w_in, w_out):
    tokens, d = x.shape
    width, ff = w_dense.shape[0], w_out.shape[0]
    heads = width // HD
    vm = pl.BlockSpec(memory_space=pltpu.VMEM)
    hbm = pl.BlockSpec(memory_space=pl.ANY)
    f32, bf16 = jnp.float32, jnp.bfloat16
    dma = pltpu.SemaphoreType.DMA
    scratch = [
        pltpu.VMEM((tokens, width), bf16),
        pltpu.VMEM((tokens, width), bf16),
        pltpu.VMEM((tokens, width), bf16),
        pltpu.VMEM((width, tokens), bf16),
        pltpu.VMEM((width, tokens), bf16),
        pltpu.VMEM((width, tokens), bf16),
        pltpu.VMEM((tokens, width), bf16),
        pltpu.VMEM((width, tokens), bf16),
        pltpu.VMEM((tokens, TILE), f32),
        pltpu.VMEM((tokens, heads * TILE), bf16),
        pltpu.VMEM((tokens, heads * TILE), bf16),
        pltpu.VMEM((heads * TILE, width), bf16),
        pltpu.VMEM((heads * TILE, width), bf16),
        pltpu.VMEM((tokens, width), f32),
        pltpu.VMEM((tokens, width), f32),
        pltpu.VMEM((width, tokens), f32),
        pltpu.VMEM((tokens, width), bf16),
        pltpu.VMEM((8, tokens), f32),
        pltpu.VMEM((8, tokens), f32),
        pltpu.VMEM((tokens, 8), f32),
        pltpu.VMEM((d, ff), bf16),
        pltpu.VMEM((ff, d), bf16),
        pltpu.VMEM((d, 3 * width), bf16),
        pltpu.VMEM((8, d), f32),
        pltpu.VMEM((TILE, ff), bf16),
        pltpu.VMEM((2, TILE, d), bf16),
        pltpu.VMEM((TILE, d), f32),
        pltpu.VMEM((2, TILE, d), f32),
        dma((3,)),
        dma,
        dma((2,)),
        dma,
        dma((2,)),
        dma((3,)),
    ]
    scratch += LineFirst.scratch() + SideFirst.scratch() + SmallSum.scratch() + TensorSum.scratch()

    def shape(*dims, dtype=f32):
        return jax.ShapeDtypeStruct(dims, dtype)

    outs = pl.pallas_call(
        functools.partial(layer_kernel, heads, dp_size),
        out_shape=(
            shape(tokens, d, dtype=bf16),
            shape(tokens, d),
            shape(ff, d),
            shape(ff, d),
            shape(width, d),
            shape(3 * width, d),
            shape(16, d),
            shape(tokens, d),
            shape(tokens, d),
            shape(ff, d),
            shape(ff, d),
            shape(width, d),
            shape(3 * width, d),
            shape(tokens, ff, dtype=bf16),
            shape(tokens, ff, dtype=bf16),
            shape(tokens, d, dtype=bf16),
        ),
        in_specs=[vm] * 4 + [hbm] * 5,
        out_specs=(hbm,) * 6 + (vm,) + (hbm,) * 9,
        scratch_shapes=scratch,
        compiler_params=pltpu.CompilerParams(
            collective_id=0, has_side_effects=True, vmem_limit_bytes=63 << 20
        ),
        name="layer",
    )(ids_row, trig, vecs, w_dense, x, cot, w_qkv, w_in, w_out)
    return outs[:7]


SLOTS = 5
STAGES = 6
CHUNK = 64
MESH_ID = pl.DeviceIdType.MESH


def z_stride(group):
    return 2 if group == 8 else 4


class Peers:
    def __init__(self, dp_size):
        stride = z_stride(dp_size)
        d, t = lax.axis_index("dp"), lax.axis_index("tensor")
        z = lax.rem(lax.div(d, stride), 4)
        base = d - z * stride
        self.y_half = lax.rem(d, 2)
        self.z_half = lax.div(z, 2)
        self.middle = jnp.logical_or(z == 1, z == 2)
        self.end = jnp.logical_or(z == 0, z == 3)
        self.y = (d + 1 - 2 * self.y_half, t)
        self.z_pair = (base + stride * (z + 1 - 2 * lax.rem(z, 2)), t)
        self.z_mid = (base + stride * (3 - z), t)
        self.z_far = (base + stride * lax.rem(z + 2, 4), t)
        self.core_half = lax.rem(t, 2)
        self.core = (d, t + 1 - 2 * lax.rem(t, 2))
        self.x = (d, lax.rem(t + 2, 4))

    def greet(self):
        barrier = pltpu.get_barrier_semaphore()
        partners = (self.y, self.z_pair, self.z_mid, self.z_far, self.core, self.x)
        for partner in partners:
            pl.semaphore_signal(barrier, inc=1, device_id=partner, device_id_type=MESH_ID)
        pl.semaphore_wait(barrier, len(partners))


def remote(src, dst, sems, index, device):
    return pltpu.make_async_remote_copy(
        src_ref=src,
        dst_ref=dst,
        send_sem=sems.at[(0,) + index],
        recv_sem=sems.at[(1,) + index],
        device_id=device,
        device_id_type=MESH_ID,
    )


class LineFirst:
    def __init__(self, peers, chunks, scratch):
        self.p, self.chunks = peers, chunks
        self.land, self.work, self.mid, self.side, self.done, self.sems, self.local = scratch

    @staticmethod
    def scratch():
        f32 = jnp.float32
        return [
            pltpu.VMEM((SLOTS, CHUNK, 1024), f32),
            pltpu.VMEM((SLOTS, CHUNK, 1024), f32),
            pltpu.VMEM((SLOTS, CHUNK // 2, 1024), f32),
            pltpu.VMEM((SLOTS, CHUNK // 2, 1024), f32),
            pltpu.VMEM((SLOTS, CHUNK, 1024), f32),
            pltpu.SemaphoreType.DMA((2, 5, SLOTS)),
            pltpu.SemaphoreType.DMA((2, SLOTS)),
        ]

    def stage(self, c, s):
        p, slot = self.p, c % SLOTS
        part, total, row, cols = self.chunks[c]
        rows, lanes = pl.ds(row, CHUNK), pl.ds(0, cols)
        half = CHUNK // 2
        own = pl.ds(pl.multiple_of(p.z_half * half, half), half)
        other = pl.ds(pl.multiple_of((1 - p.z_half) * half, half), half)
        land, work = self.land.at[slot, :, lanes], self.work.at[slot, :, lanes]
        mid, side = self.mid.at[slot, :, lanes], self.side.at[slot, :, lanes]
        done = self.done.at[slot, :, lanes]
        inward = functools.partial(remote, part.at[rows], land, self.sems, (0, slot), p.z_pair)
        across = functools.partial(remote, work.at[other], mid, self.sems, (1, slot), p.z_mid)
        beside = functools.partial(remote, work.at[own], side, self.sems, (2, slot), p.y)
        back = functools.partial(remote, done.at[own], done.at[own], self.sems, (3, slot), p.z_mid)
        outward = functools.partial(remote, done, total.at[rows], self.sems, (4, slot), p.z_pair)
        fetch = functools.partial(pltpu.make_async_copy, part.at[rows], work, self.local.at[0, slot])
        store = functools.partial(pltpu.make_async_copy, done, total.at[rows], self.local.at[1, slot])

        if s == 0:

            @pl.when(p.end)
            def _():
                inward().start()

            @pl.when(p.middle)
            def _():
                fetch().start()

        if s == 5:

            @pl.when(p.end)
            def _():
                outward().wait_recv()
                inward().wait_send()

        if s > 0:

            @pl.when(p.middle)
            def _():
                if s == 1:
                    fetch().wait()
                    inward().wait_recv()
                    work[...] += land[...]
                    across().start()
                if s == 2:
                    across().wait_recv()
                    work[own] += mid[...]
                    beside().start()
                if s == 3:
                    beside().wait_recv()
                    done[own] = work[own] + side[...]
                    back().start()
                if s == 4:
                    back().wait_recv()
                    outward().start()
                    store().start()
                if s == 5:
                    for copy in (across, beside, back, outward):
                        copy().wait_send()
                    store().wait()

    def tick(self, t):
        for s in reversed(range(STAGES)):
            if 0 <= t - s < len(self.chunks):
                self.stage(t - s, s)


class SideFirst:
    def __init__(self, peers, chunks, scratch):
        self.p, self.chunks = peers, chunks
        self.land, self.work, self.line, self.mid, self.done, self.sems, self.local = scratch

    @staticmethod
    def scratch():
        return [pltpu.VMEM((SLOTS, CHUNK // 2, 1024), jnp.float32)] * 5 + [
            pltpu.SemaphoreType.DMA((2, 5, SLOTS)),
            pltpu.SemaphoreType.DMA((2, SLOTS)),
        ]

    def stage(self, c, s):
        p, slot = self.p, c % SLOTS
        part, total, row, cols = self.chunks[c]
        lanes, half = pl.ds(0, cols), CHUNK // 2
        own = pl.ds(pl.multiple_of(row + p.y_half * half, half), half)
        other = pl.ds(pl.multiple_of(row + (1 - p.y_half) * half, half), half)
        land, work = self.land.at[slot, :, lanes], self.work.at[slot, :, lanes]
        line, mid = self.line.at[slot, :, lanes], self.mid.at[slot, :, lanes]
        done = self.done.at[slot, :, lanes]
        beside = functools.partial(remote, part.at[other], land, self.sems, (0, slot), p.y)
        inward = functools.partial(remote, work, line, self.sems, (1, slot), p.z_pair)
        across = functools.partial(remote, work, mid, self.sems, (2, slot), p.z_mid)
        outward = functools.partial(remote, done, done, self.sems, (3, slot), p.z_pair)
        back = functools.partial(remote, done, total.at[own], self.sems, (4, slot), p.y)
        fetch = functools.partial(pltpu.make_async_copy, part.at[own], work, self.local.at[0, slot])
        store = functools.partial(pltpu.make_async_copy, done, total.at[own], self.local.at[1, slot])

        if s == 0:
            beside().start()
            fetch().start()
        if s == 1:
            fetch().wait()
            beside().wait_recv()
            work[...] += land[...]

            @pl.when(p.end)
            def _():
                inward().start()

        if s in (2, 3):

            @pl.when(p.middle)
            def _():
                if s == 2:
                    inward().wait_recv()
                    work[...] += line[...]
                    across().start()
                if s == 3:
                    across().wait_recv()
                    done[...] = work[...] + mid[...]
                    outward().start()

        if s == 4:

            @pl.when(p.end)
            def _():
                outward().wait_recv()

            back().start()
            store().start()
        if s == 5:
            back().wait()
            beside().wait_send()
            store().wait()

            @pl.when(p.end)
            def _():
                inward().wait_send()

            @pl.when(p.middle)
            def _():
                across().wait_send()
                outward().wait_send()

    def tick(self, t):
        for s in reversed(range(STAGES)):
            if 0 <= t - s < len(self.chunks):
                self.stage(t - s, s)


class SmallSum:
    def __init__(self, peers, scratch):
        self.p = peers
        self.kept, self.got, self.sems = scratch

    @staticmethod
    def scratch():
        return [
            pltpu.VMEM((6, 8, 1024), jnp.float32),
            pltpu.VMEM((5, 8, 1024), jnp.float32),
            pltpu.SemaphoreType.DMA((2, 5)),
        ]

    def copy(self, s):
        p = self.p
        partner = (p.y, p.z_pair, p.z_far, p.core, p.x)[s]
        return remote(self.kept.at[s], self.got.at[s], self.sems, (s,), partner)

    def start(self, rows):
        self.kept[0] = rows
        self.copy(0).start()

    def step(self, s):
        self.copy(s).wait()
        self.kept[s + 1] = self.kept[s] + self.got[s]
        if s < 4:
            self.copy(s + 1).start()


class TensorSum:
    def __init__(self, peers, chunks, arrays, scratch):
        self.p, self.chunks = peers, chunks
        self.x, self.cot, self.vecs, self.output, self.grad_input = arrays
        self.land, self.work, self.mid, self.done, self.sems, self.local = scratch[:6]
        self.rows_x, self.rows_cot, self.rows_out, self.rows_grad, self.sem = scratch[6:]
        self.push = {}

    @staticmethod
    def scratch():
        f32, bf16 = jnp.float32, jnp.bfloat16
        return [
            pltpu.VMEM((2, TILE // 2, 1024), f32),
            pltpu.VMEM((3, TILE // 2, 1024), f32),
            pltpu.VMEM((4, TILE // 2, 1024), f32),
            pltpu.VMEM((2, TILE, 1024), f32),
            pltpu.SemaphoreType.DMA((2, 3, 4)),
            pltpu.SemaphoreType.DMA((3,)),
            pltpu.VMEM((TILE, 1024), bf16),
            pltpu.VMEM((TILE, 1024), bf16),
            pltpu.VMEM((TILE, 1024), bf16),
            pltpu.VMEM((TILE, 1024), f32),
            pltpu.SemaphoreType.DMA((4,)),
        ]

    def settle(self):
        for copy in self.push.values():
            copy.wait()
        self.push = {}

    def stage(self, c, s):
        p, half = self.p, TILE // 2
        part, row, backward = self.chunks[c]
        rows = pl.ds(row, TILE)
        own = pl.ds(pl.multiple_of(row + p.core_half * half, half), half)
        other = pl.ds(pl.multiple_of(row + (1 - p.core_half) * half, half), half)
        own_done = self.done.at[c % 2, pl.ds(pl.multiple_of(p.core_half * half, half), half)]
        land, work, mid = self.land.at[c % 2], self.work.at[c % 3], self.mid.at[c % 4]
        beside = functools.partial(remote, part.at[other], land, self.sems, (0, c % 2), p.core)
        across = functools.partial(remote, work, mid, self.sems, (1, c % 4), p.x)
        back = functools.partial(remote, own_done, own_done, self.sems, (2, c % 2), p.core)
        fetch = functools.partial(pltpu.make_async_copy, part.at[own], work, self.local.at[c % 3])
        get_x = functools.partial(
            pltpu.make_async_copy, self.x.at[rows], self.rows_x, self.sem.at[0]
        )
        get_cot = functools.partial(
            pltpu.make_async_copy, self.cot.at[rows], self.rows_cot, self.sem.at[1]
        )
        if s == 0:
            beside().start()
            fetch().start()
        if s == 1:
            fetch().wait()
            beside().wait()
            work[...] += land[...]
            across().start()
        if s == 2:
            get_x().start()
            if backward:
                get_cot().start()
            across().wait()
            own_done[...] = work[...] + mid[...]
            back().start()
        if s == 3:
            get_x().wait()
            if backward:
                get_cot().wait()
            back().wait()
            if backward in self.push:
                self.push.pop(backward).wait()
            total = self.done[c % 2]
            if backward:
                standard, inv_std = standardize(self.rows_x[...])
                scaled = total * self.vecs[0:1]
                inner = (
                    scaled
                    - jnp.mean(scaled, axis=1, keepdims=True)
                    - standard * jnp.mean(scaled * standard, axis=1, keepdims=True)
                )
                self.rows_grad[...] = self.rows_cot[...].astype(jnp.float32) + inv_std * inner
                copy = pltpu.make_async_copy(
                    self.rows_grad, self.grad_input.at[rows], self.sem.at[3]
                )
            else:
                biases = self.vecs[3:4] + self.vecs[4:5]
                result = self.rows_x[...].astype(jnp.float32) + total + biases
                self.rows_out[...] = result.astype(jnp.bfloat16)
                copy = pltpu.make_async_copy(self.rows_out, self.output.at[rows], self.sem.at[2])
            copy.start()
            self.push[backward] = copy

    def tick(self, t):
        for s, delay in reversed(list(enumerate(X_DELAYS))):
            if 0 <= t - delay < len(self.chunks):
                self.stage(t - delay, s)


def chunk_lists(parts, totals):
    ways = ([], [])
    for turn, (part, total) in enumerate(zip(parts, totals)):
        for i in range(part.shape[0] // CHUNK):
            ways[(turn if turn < 2 else i) % 2].append((part, total, i * CHUNK, part.shape[1]))
    return ways


def rest_groups(dp_size):
    stride = z_stride(dp_size)
    places = np.arange(dp_size).reshape(-1, 4, stride // 2, 2)
    return places.transpose(1, 3, 0, 2).reshape(8, -1).tolist()


def on_device(
    dp_size,
    layer_input,
    positions,
    block_ids,
    ln_gain,
    ln_bias,
    w_qkv,
    b_qkv,
    w_dense,
    b_dense,
    w_in,
    b_in,
    w_out,
    b_out,
    cotangent,
):
    d = layer_input.shape[1]
    width = w_dense.shape[0]
    heads = width // HD
    frequency = rotary_base ** (-jnp.arange(0, ROT, 2).astype(jnp.float32) / ROT)
    phases = frequency[:, None] * positions.astype(jnp.float32)[None, :]
    trig = jnp.concatenate([jnp.cos(phases), jnp.sin(phases)], axis=0)
    bias = b_qkv.reshape(heads, 3, HD).transpose(1, 0, 2).reshape(3 * width)
    none = jnp.zeros((d,), jnp.float32)
    rows = [ln_gain, ln_bias, b_in, b_dense, b_out, jnp.pad(bias, (0, d - 3 * width)), none, none]
    output, grad_input, *sums = layer_call(
        dp_size,
        block_ids.astype(jnp.float32)[None, :],
        trig,
        jnp.stack(rows),
        w_dense,
        layer_input,
        cotangent,
        w_qkv,
        w_in,
        w_out,
    )
    if dp_size > 8:
        sums = lax.psum(sums, "dp", axis_index_groups=rest_groups(dp_size))
    grad_w_out, grad_w_in, grad_w_dense, grad_w_qkv, small = sums
    grad_w_qkv = grad_w_qkv.reshape(3, heads, HD, d).transpose(3, 1, 0, 2).reshape(d, 3 * width)
    grad_b_qkv = small[4, : 3 * width].reshape(3, heads, HD).transpose(1, 0, 2).reshape(3 * width)
    bias_grad = small[2]
    return (
        output,
        grad_input,
        small[8],
        small[9],
        grad_w_qkv,
        grad_b_qkv,
        grad_w_dense,
        bias_grad,
        grad_w_in.T,
        small[3],
        grad_w_out,
        bias_grad,
    )


def solution(mesh):
    in_specs = (
        P("dp", None),
        P("dp"),
        P("dp"),
        P(),
        P(),
        P(None, "tensor"),
        P("tensor"),
        P("tensor", None),
        P(),
        P(None, "tensor"),
        P("tensor"),
        P("tensor", None),
        P(),
        P("dp", None),
    )
    out_specs = (
        P("dp", None),
        P("dp", None),
        P(),
        P(),
        P(None, "tensor"),
        P("tensor"),
        P("tensor", None),
        P(),
        P(None, "tensor"),
        P("tensor"),
        P("tensor", None),
        P(),
    )
    return jax.shard_map(
        functools.partial(on_device, mesh.shape["dp"]), mesh=mesh, in_specs=in_specs, out_specs=out_specs, check_vma=False
    )
```

```python
import functools

import jax
import jax.numpy as jnp
import numpy as np
from jax import lax
from jax.experimental import pallas as pl
from jax.experimental.pallas import tpu as pltpu
from jax.sharding import PartitionSpec as P

HD = 64
ROT = 16
TILE = 256

eps = 1e-05
rotary_base = 10000.0
NT = (((1,), (1,)), ((), ()))
TN = (((0,), (0,)), ((), ()))
NN = (((1,), (0,)), ((), ()))


def mm(a, b, dims=NN):
    return lax.dot_general(a, b, dims, preferred_element_type=jnp.float32)


def layer_kernel(
    heads,
    dp_size,
    ids_row,
    trig,
    vecs,
    w_dense,
    x_hbm,
    cot_hbm,
    w_qkv_hbm,
    w_in_hbm,
    w_out_hbm,
    output,
    grad_input,
    sum_w_out,
    sum_w_in,
    sum_w_dense,
    sum_w_qkv,
    small_sum,
    out_part,
    dnorm_part,
    gw_out,
    gw_in,
    gw_dense,
    gw_qkv,
    act_hbm,
    dh_hbm,
    q,
    k,
    v,
    q_t,
    k_t,
    v_t,
    do,
    do_t,
    scores,
    probs,
    normed,
    wide,
    stack_a,
    stack_b,
    dk,
    dv,
    dq_t,
    mixed,
    lse,
    delta,
    ids_col,
    w_in,
    w_out,
    w_cols,
    rows_sum,
    stage_h,
    stage_x,
    stage_out,
    stage_w,
    big_sem,
    h_sem,
    x_sem,
    out_sem,
    w_sem,
    spill_sem,
    *comm,
):
    tokens, d = x_hbm.shape
    tiles = tokens // TILE
    width = heads * HD
    ff = w_out.shape[0]
    f32, bf16 = jnp.float32, jnp.bfloat16
    parts = len(LineFirst.scratch())
    peers = Peers(dp_size)
    line, side = chunk_lists(
        (gw_out, gw_in, gw_dense, gw_qkv), (sum_w_out, sum_w_in, sum_w_dense, sum_w_qkv)
    )
    line_sum = LineFirst(peers, line, comm[:parts])
    side_sum = SideFirst(peers, side, comm[parts : 2 * parts])
    little = SmallSum(peers, comm[2 * parts : 2 * parts + 3])
    tensor_sum = TensorSum(
        peers,
        [(out_part, t * TILE, False) for t in range(tiles)]
        + [(dnorm_part, t * TILE, True) for t in reversed(range(tiles))],
        (x_hbm, cot_hbm, vecs, output, grad_input),
        comm[2 * parts + 3 :],
    )
    rounds = max(len(line), len(side)) + STAGES - 1
    state = {"d": 0, "x": 0, "made": 0, "push": None, "ready": 0, "due_d": 0.0, "due_x": 0.0}

    def settle():
        if state["push"] is not None:
            state["push"].wait()
            state["push"] = None

    def tick_x():
        n, last = state["x"], len(tensor_sum.chunks)
        if n < min(state["made"], last) or (state["made"] == last and n < last + X_DELAYS[-1]):
            settle()
            tensor_sum.tick(n)
            state["x"] += 1
            return True
        return False

    def tick_d():
        n = state["d"]
        if n < (state["ready"] if state["ready"] < len(line) else rounds):
            line_sum.tick(n)
            side_sum.tick(n)
            state["d"] += 1
            return True
        return False

    def worked(us):
        for way, pace, step in (("due_d", D_PACE, tick_d), ("due_x", X_PACE, tick_x)):
            state[way] = min(state[way] + us, 2 * pace)
            if state[way] >= pace and step():
                state[way] -= pace

    def begin(src, dst, sem):
        copy = pltpu.make_async_copy(src, dst, sem)
        copy.start()
        return copy

    def tile_rows(t):
        return pl.ds(t * TILE, TILE)

    lane_head = lax.broadcasted_iota(jnp.int32, (1, width), 1) >> 6
    row_head = lax.broadcasted_iota(jnp.int32, (width, 1), 0) >> 6

    def head_lanes(h):
        return (lane_head == h).astype(f32).astype(bf16)

    def head_rows(h):
        return (row_head == h).astype(f32).astype(bf16)

    peers.greet()
    qkv_copy = begin(w_qkv_hbm, w_in.at[:, pl.ds(0, 3 * width)], big_sem.at[0])
    x_copy = begin(x_hbm.at[tile_rows(0)], stage_x.at[0], x_sem.at[0])
    qkv_copy.wait()
    for part in range(3):
        pieces = [w_in[:, (3 * h + part) * HD : (3 * h + part + 1) * HD] for h in range(heads)]
        w_cols[:, part * width : (part + 1) * width] = jnp.concatenate(pieces, axis=1)

    gain, shift = vecs[0:1], vecs[1:2]
    for t in range(tiles):
        x_copy.wait()
        if t + 1 < tiles:
            slot = (t + 1) % 2
            next_copy = begin(x_hbm.at[tile_rows(t + 1)], stage_x.at[slot], x_sem.at[slot])
        if t == 0:
            w_in_copy = begin(w_in_hbm, w_in, big_sem.at[0])
        if t == 1:
            cot_copy = begin(cot_hbm, wide, big_sem.at[1])
        if t == 3:
            w_out_copy = begin(w_out_hbm, w_out, big_sem.at[2])
        standard, _ = standardize(stage_x[t % 2])
        normed[tile_rows(t)] = (standard * gain + shift).astype(bf16)
        x_copy = next_copy
        ids_tile = jnp.broadcast_to(ids_row[:, t * TILE : (t + 1) * TILE], (8, TILE))
        ids_col[tile_rows(t)] = ids_tile.T

    act_block, dh_block = mixed, do
    rows_sum[...] = jnp.zeros_like(rows_sum)
    cot_copy.wait()
    w_in_copy.wait()
    w_out_copy.wait()
    spills, puts = [], []

    def put_grad(value, part, row, slot):
        size = value.shape[0]
        stage_w[slot, 0:size] = value
        return begin(stage_w.at[slot, pl.ds(0, size)], part.at[pl.ds(row, size)], w_sem.at[slot])

    for c in range(ff // TILE):
        units = pl.ds(c * TILE, TILE)
        for copy in spills:
            copy.wait()
        for start in range(0, tokens, 2 * TILE):
            rows = pl.ds(start, 2 * TILE)
            hidden = mm(normed[rows], w_in[:, units]) + vecs[2:3, units]
            normal_cdf = 0.5 * (1.0 + lax.erf(hidden * 0.7071067811865476))
            act_block[rows] = (hidden * normal_cdf).astype(bf16)
            normal_pdf = jnp.exp(-0.5 * hidden * hidden) * 0.3989422804014327
            d_active = mm(wide[rows], w_out[units], NT)
            d_hidden = (d_active * (normal_cdf + hidden * normal_pdf)).astype(bf16)
            dh_block[rows] = d_hidden
            rows_sum[3:4, units] += jnp.sum(d_hidden.astype(f32), axis=0, keepdims=True)
        spills = [
            begin(act_block, act_hbm.at[:, units], spill_sem.at[0]),
            begin(dh_block, dh_hbm.at[:, units], spill_sem.at[1]),
        ]
        worked(3.6)
        puts = [
            put_grad(mm(act_block[...], wide[...], TN), gw_out, c * TILE, 0),
            put_grad(mm(dh_block[...], normed[...], TN), gw_in, c * TILE, 1),
        ]
        for copy in puts:
            copy.wait()
        state["ready"] += TILE // CHUNK
        worked(2.4)
    for copy in spills:
        copy.wait()

    half = ROT // 2
    still = jnp.ones((HD - ROT, TILE), f32)
    none = jnp.zeros((HD - ROT, TILE), f32)
    blank = jnp.zeros((half, TILE), f32)

    def lane_tables(cols):
        cosine, sine = trig[0:half, cols], trig[half : 2 * half, cols]
        cos_head = [cosine, cosine, still]
        low_head = [-sine, blank, none]
        high_head = [blank, sine, none]
        return tuple(jnp.concatenate(t + t, axis=0).T for t in (cos_head, low_head, high_head))

    def turn(value, tables, sign):
        cos_t, low_t, high_t = tables
        halves = []
        for part in range(value.shape[1] // 128):
            g = value[:, part * 128 : (part + 1) * 128]
            moved = pltpu.roll(g, 120, 1) * low_t + pltpu.roll(g, 8, 1) * high_t
            halves.append(g * cos_t + sign * moved)
        return jnp.concatenate(halves, axis=1)

    for t in range(tiles):
        rows = tile_rows(t)
        tables = lane_tables(rows)
        projected = mm(normed[rows], w_cols[...]) + vecs[5:6, 0 : 3 * width]
        query = turn(projected[:, 0:width], tables, 1.0).astype(bf16) * HD**-0.5
        key = turn(projected[:, width : 2 * width], tables, 1.0).astype(bf16)
        value = projected[:, 2 * width :].astype(bf16)
        d_out = mm(wide[rows], w_dense[...], NT).astype(bf16)
        q[rows], k[rows], v[rows], do[rows] = query, key, value, d_out
        q_t[:, rows], k_t[:, rows], v_t[:, rows], do_t[:, rows] = query.T, key.T, value.T, d_out.T
        rows_sum[2:3] += jnp.sum(wide[rows].astype(f32), axis=0, keepdims=True)
        worked(0.7)

    def send_out(value, part, rows):
        settle()
        stage_out[...] = value
        state["push"] = begin(stage_out, part.at[rows], out_sem)
        state["made"] += 1

    def span(i):
        return min(i + 2, tiles) * TILE

    for i in range(tiles):
        n, cols = span(i), tile_rows(i)
        fetch = begin(act_hbm.at[cols], stage_h, h_sem)

        def head_forward(h, _):
            rows = pl.ds(pl.multiple_of(h * HD, HD), HD)
            q_head = q_t[:, cols] * head_rows(h)
            top = None
            for start in range(0, n, TILE):
                keys = pl.ds(start, TILE)
                tile_scores = mm(k[keys], q_head)
                if start >= i * TILE:
                    allowed = ids_col[keys, 0:1] <= ids_row[:, cols]
                    tile_scores = jnp.where(allowed, tile_scores, -1e30)
                scores[keys] = tile_scores
                tile_top = jnp.max(tile_scores, axis=0, keepdims=True)
                top = tile_top if top is None else jnp.maximum(top, tile_top)
            total = jnp.zeros_like(top)
            for start in range(0, n, TILE):
                keys = pl.ds(start, TILE)
                weights = jnp.exp(scores[keys] - top)
                total += jnp.sum(weights, axis=0, keepdims=True)
                probs[keys, 0:TILE] = weights.astype(bf16)
            head_out = mm(v_t[rows, 0:n], probs[0:n, 0:TILE]) / total
            lse[pl.ds(h, 1), cols] = top + jnp.log(total)
            delta[pl.ds(h, 1), cols] = jnp.sum(
                head_out * do_t[rows, cols].astype(f32), axis=0, keepdims=True
            )
            dq_t[rows, cols] = head_out
            return 0

        lax.fori_loop(0, heads, head_forward, 0)
        mixed_tile = dq_t[:, cols].T.astype(bf16)
        mixed[cols] = mixed_tile
        fetch.wait()
        send_out(mm(mixed_tile, w_dense[...]) + mm(stage_h[...], w_out[...]), out_part, cols)
        worked(1.1 * n / TILE + 0.6)

    put_grad(mm(mixed[...], wide[...], TN), gw_dense, 0, 0).wait()
    state["ready"] += width // (2 * CHUNK)
    worked(0.8)

    def finish(pair, t, copies):
        rows = tile_rows(t)
        lanes = pl.ds(pair * PAIR, PAIR)
        tables = lane_tables(rows)
        dq_tile = turn(dq_t[lanes, rows].T * (HD**-0.5), tables, -1.0).astype(bf16)
        dk_tile = turn(dk[rows, lanes], tables, -1.0).astype(bf16)
        dv_tile = dv[rows, lanes].astype(bf16)
        for part, (held, piece) in enumerate(((q, dq_tile), (k, dk_tile), (v, dv_tile))):
            held[rows, lanes] = piece
            place = pl.ds(part * width + pair * PAIR, PAIR)
            rows_sum[4:5, place] += jnp.sum(piece.astype(f32), axis=0, keepdims=True)
        if pair < width // PAIR - 1:
            return
        for copy in copies:
            copy.wait()
        d_tile = mm(stage_h[...], w_in[...], NT)
        for part, held in enumerate((q, k, v)):
            d_tile += mm(held[rows], w_cols[:, part * width : (part + 1) * width], NT)
        send_out(d_tile, dnorm_part, rows)
        standard, _ = standardize(stage_x[0])
        rows_sum[0:1] += jnp.sum(d_tile * standard, axis=0, keepdims=True)
        rows_sum[1:2] += jnp.sum(d_tile, axis=0, keepdims=True)

    def fetches(t):
        rows = tile_rows(t)
        return (
            begin(dh_hbm.at[rows], stage_h, h_sem),
            begin(x_hbm.at[rows], stage_x.at[0], x_sem.at[0]),
        )

    lane_in_pair = lax.broadcasted_iota(jnp.int32, (1, PAIR), 1) >> 6
    row_in_pair = lax.broadcasted_iota(jnp.int32, (PAIR, 1), 0) >> 6
    for pair in range(width // PAIR):
        last = pair == width // PAIR - 1
        lanes = pl.ds(pair * PAIR, PAIR)
        for i in reversed(range(tiles)):
            n, cols = span(i), tile_rows(i)
            copies = fetches(i + 1) if last and i < tiles - 1 else None
            for j in range(2):
                own = (lane_in_pair == j).astype(f32).astype(bf16)
                stack_a[j * TILE : (j + 1) * TILE] = do[cols, lanes] * own
                stack_b[j * TILE : (j + 1) * TILE] = q[cols, lanes] * own

            def head_backward(j, _):
                h = 2 * pair + j
                rows = pl.ds(pl.multiple_of(h * HD, HD), HD)
                block = pl.ds(pl.multiple_of(j * TILE, TILE), TILE)
                d_block = pl.ds(pl.multiple_of((2 + j) * TILE, TILE), TILE)
                own = (row_in_pair == j).astype(f32).astype(bf16)
                q_head, do_head = q_t[lanes, cols] * own, do_t[lanes, cols] * own
                top, row_delta = lse[pl.ds(h, 1), cols], delta[pl.ds(h, 1), cols]
                for start in range(0, n, TILE):
                    keys = pl.ds(start, TILE)
                    tile_scores = mm(k[keys, lanes], q_head)
                    if start >= i * TILE:
                        allowed = ids_col[keys, 0:1] <= ids_row[:, cols]
                        tile_scores = jnp.where(allowed, tile_scores, -1e30)
                    weights = jnp.exp(tile_scores - top)
                    wide[keys, block] = weights.astype(bf16)
                    d_tile = weights * (mm(v[keys, lanes], do_head) - row_delta)
                    wide[keys, d_block] = d_tile.astype(bf16)
                dq_t[rows, cols] = mm(k_t[rows, 0:n], wide[0:n, d_block])
                return 0

            lax.fori_loop(0, 2, head_backward, 0)
            worked(0.5 * n / TILE)
            for grad, first, right in ((dv, 0, stack_a), (dk, 2 * TILE, stack_b)):
                for start in range(0, n, 2 * TILE):
                    keys = pl.ds(start, min(2 * TILE, n - start))
                    term = mm(wide[keys, pl.ds(first, 2 * TILE)], right[...])
                    grad[keys, lanes] = term if i == tiles - 1 else grad[keys, lanes] + term
            if i < tiles - 1:
                finish(pair, i + 1, copies)
            worked(0.15 * n / TILE + (1.4 if last else 0.5))
        finish(pair, 0, fetches(0) if last else None)
        if last:
            little.start(rows_sum[...])
        for part, held in enumerate((q, k, v)):
            term = mm(held[:, lanes], normed[...], TN)
            put_grad(term, gw_qkv, part * width + pair * PAIR, 0).wait()
        state["ready"] += 3 * PAIR // (2 * CHUNK)
        worked(2.5)

    for s in range(5):
        worked(D_PACE)
        little.step(s)
    small_sum[0:8] = little.kept[3]
    small_sum[8:16] = little.kept[5]
    while state["d"] < rounds:
        worked(D_PACE)
    while tick_x():
        pass
    tensor_sum.settle()


PAIR = 2 * HD
D_PACE = 7.6
X_PACE = 11.4
X_DELAYS = (0, 1, 3, 4)


def standardize(rows):
    centred = rows.astype(jnp.float32)
    centred = centred - jnp.mean(centred, axis=1, keepdims=True)
    inv_std = lax.rsqrt(jnp.mean(centred * centred, axis=1, keepdims=True) + eps)
    return centred * inv_std, inv_std


def layer_call(dp_size, ids_row, trig, vecs, w_dense, x, cot, w_qkv, w_in, w_out):
    tokens, d = x.shape
    width, ff = w_dense.shape[0], w_out.shape[0]
    heads = width // HD
    vm = pl.BlockSpec(memory_space=pltpu.VMEM)
    hbm = pl.BlockSpec(memory_space=pl.ANY)
    f32, bf16 = jnp.float32, jnp.bfloat16
    dma = pltpu.SemaphoreType.DMA
    scratch = [
        pltpu.VMEM((tokens, width), bf16),
        pltpu.VMEM((tokens, width), bf16),
        pltpu.VMEM((tokens, width), bf16),
        pltpu.VMEM((width, tokens), bf16),
        pltpu.VMEM((width, tokens), bf16),
        pltpu.VMEM((width, tokens), bf16),
        pltpu.VMEM((tokens, width), bf16),
        pltpu.VMEM((width, tokens), bf16),
        pltpu.VMEM((tokens, TILE), f32),
        pltpu.VMEM((tokens, TILE), bf16),
        pltpu.VMEM((tokens, d), bf16),
        pltpu.VMEM((tokens, d), bf16),
        pltpu.VMEM((2 * TILE, PAIR), bf16),
        pltpu.VMEM((2 * TILE, PAIR), bf16),
        pltpu.VMEM((tokens, width), f32),
        pltpu.VMEM((tokens, width), f32),
        pltpu.VMEM((width, tokens), f32),
        pltpu.VMEM((tokens, width), bf16),
        pltpu.VMEM((8, tokens), f32),
        pltpu.VMEM((8, tokens), f32),
        pltpu.VMEM((tokens, 8), f32),
        pltpu.VMEM((d, ff), bf16),
        pltpu.VMEM((ff, d), bf16),
        pltpu.VMEM((d, 3 * width), bf16),
        pltpu.VMEM((8, d), f32),
        pltpu.VMEM((TILE, ff), bf16),
        pltpu.VMEM((2, TILE, d), bf16),
        pltpu.VMEM((TILE, d), f32),
        pltpu.VMEM((2, TILE, d), f32),
        dma((3,)),
        dma,
        dma((2,)),
        dma,
        dma((2,)),
        dma((2,)),
    ]
    scratch += LineFirst.scratch() + SideFirst.scratch() + SmallSum.scratch() + TensorSum.scratch()

    def shape(*dims, dtype=f32):
        return jax.ShapeDtypeStruct(dims, dtype)

    outs = pl.pallas_call(
        functools.partial(layer_kernel, heads, dp_size),
        out_shape=(
            shape(tokens, d, dtype=bf16),
            shape(tokens, d),
            shape(ff, d),
            shape(ff, d),
            shape(width, d),
            shape(3 * width, d),
            shape(16, d),
            shape(tokens, d),
            shape(tokens, d),
            shape(ff, d),
            shape(ff, d),
            shape(width, d),
            shape(3 * width, d),
            shape(tokens, ff, dtype=bf16),
            shape(tokens, ff, dtype=bf16),
        ),
        in_specs=[vm] * 4 + [hbm] * 5,
        out_specs=(hbm,) * 6 + (vm,) + (hbm,) * 8,
        scratch_shapes=scratch,
        compiler_params=pltpu.CompilerParams(
            collective_id=0, has_side_effects=True, vmem_limit_bytes=63 << 20
        ),
        name="layer",
    )(ids_row, trig, vecs, w_dense, x, cot, w_qkv, w_in, w_out)
    return outs[:7]


SLOTS = 5
STAGES = 6
CHUNK = 64
MESH_ID = pl.DeviceIdType.MESH


def z_stride(group):
    return 2 if group == 8 else 4


class Peers:
    def __init__(self, dp_size):
        stride = z_stride(dp_size)
        d, t = lax.axis_index("dp"), lax.axis_index("tensor")
        z = lax.rem(lax.div(d, stride), 4)
        base = d - z * stride
        self.y_half = lax.rem(d, 2)
        self.z_half = lax.div(z, 2)
        self.middle = jnp.logical_or(z == 1, z == 2)
        self.end = jnp.logical_or(z == 0, z == 3)
        self.y = (d + 1 - 2 * self.y_half, t)
        self.z_pair = (base + stride * (z + 1 - 2 * lax.rem(z, 2)), t)
        self.z_mid = (base + stride * (3 - z), t)
        self.z_far = (base + stride * lax.rem(z + 2, 4), t)
        self.core_half = lax.rem(t, 2)
        self.core = (d, t + 1 - 2 * lax.rem(t, 2))
        self.x = (d, lax.rem(t + 2, 4))

    def greet(self):
        barrier = pltpu.get_barrier_semaphore()
        partners = (self.y, self.z_pair, self.z_mid, self.z_far, self.core, self.x)
        for partner in partners:
            pl.semaphore_signal(barrier, inc=1, device_id=partner, device_id_type=MESH_ID)
        pl.semaphore_wait(barrier, len(partners))


def remote(src, dst, sems, index, device):
    return pltpu.make_async_remote_copy(
        src_ref=src,
        dst_ref=dst,
        send_sem=sems.at[(0,) + index],
        recv_sem=sems.at[(1,) + index],
        device_id=device,
        device_id_type=MESH_ID,
    )


class LineFirst:
    def __init__(self, peers, chunks, scratch):
        self.p, self.chunks = peers, chunks
        self.land, self.work, self.mid, self.side, self.done, self.sems, self.local = scratch

    @staticmethod
    def scratch():
        f32 = jnp.float32
        return [
            pltpu.VMEM((SLOTS, CHUNK, 1024), f32),
            pltpu.VMEM((SLOTS, CHUNK, 1024), f32),
            pltpu.VMEM((SLOTS, CHUNK // 2, 1024), f32),
            pltpu.VMEM((SLOTS, CHUNK // 2, 1024), f32),
            pltpu.VMEM((SLOTS, CHUNK, 1024), f32),
            pltpu.SemaphoreType.DMA((2, 5, SLOTS)),
            pltpu.SemaphoreType.DMA((2, SLOTS)),
        ]

    def stage(self, c, s):
        p, slot = self.p, c % SLOTS
        part, total, row, cols = self.chunks[c]
        rows, lanes = pl.ds(row, CHUNK), pl.ds(0, cols)
        half = CHUNK // 2
        own = pl.ds(pl.multiple_of(p.z_half * half, half), half)
        other = pl.ds(pl.multiple_of((1 - p.z_half) * half, half), half)
        land, work = self.land.at[slot, :, lanes], self.work.at[slot, :, lanes]
        mid, side = self.mid.at[slot, :, lanes], self.side.at[slot, :, lanes]
        done = self.done.at[slot, :, lanes]
        inward = functools.partial(remote, part.at[rows], land, self.sems, (0, slot), p.z_pair)
        across = functools.partial(remote, work.at[other], mid, self.sems, (1, slot), p.z_mid)
        beside = functools.partial(remote, work.at[own], side, self.sems, (2, slot), p.y)
        back = functools.partial(remote, done.at[own], done.at[own], self.sems, (3, slot), p.z_mid)
        outward = functools.partial(remote, done, total.at[rows], self.sems, (4, slot), p.z_pair)
        fetch = functools.partial(pltpu.make_async_copy, part.at[rows], work, self.local.at[0, slot])
        store = functools.partial(pltpu.make_async_copy, done, total.at[rows], self.local.at[1, slot])

        if s == 0:

            @pl.when(p.end)
            def _():
                inward().start()

            @pl.when(p.middle)
            def _():
                fetch().start()

        if s == 5:

            @pl.when(p.end)
            def _():
                outward().wait_recv()
                inward().wait_send()

        if s > 0:

            @pl.when(p.middle)
            def _():
                if s == 1:
                    fetch().wait()
                    inward().wait_recv()
                    work[...] += land[...]
                    across().start()
                if s == 2:
                    across().wait_recv()
                    work[own] += mid[...]
                    beside().start()
                if s == 3:
                    beside().wait_recv()
                    done[own] = work[own] + side[...]
                    back().start()
                if s == 4:
                    back().wait_recv()
                    outward().start()
                    store().start()
                if s == 5:
                    for copy in (across, beside, back, outward):
                        copy().wait_send()
                    store().wait()

    def tick(self, t):
        for s in reversed(range(STAGES)):
            if 0 <= t - s < len(self.chunks):
                self.stage(t - s, s)


class SideFirst:
    def __init__(self, peers, chunks, scratch):
        self.p, self.chunks = peers, chunks
        self.land, self.work, self.line, self.mid, self.done, self.sems, self.local = scratch

    @staticmethod
    def scratch():
        return [pltpu.VMEM((SLOTS, CHUNK // 2, 1024), jnp.float32)] * 5 + [
            pltpu.SemaphoreType.DMA((2, 5, SLOTS)),
            pltpu.SemaphoreType.DMA((2, SLOTS)),
        ]

    def stage(self, c, s):
        p, slot = self.p, c % SLOTS
        part, total, row, cols = self.chunks[c]
        lanes, half = pl.ds(0, cols), CHUNK // 2
        own = pl.ds(pl.multiple_of(row + p.y_half * half, half), half)
        other = pl.ds(pl.multiple_of(row + (1 - p.y_half) * half, half), half)
        land, work = self.land.at[slot, :, lanes], self.work.at[slot, :, lanes]
        line, mid = self.line.at[slot, :, lanes], self.mid.at[slot, :, lanes]
        done = self.done.at[slot, :, lanes]
        beside = functools.partial(remote, part.at[other], land, self.sems, (0, slot), p.y)
        inward = functools.partial(remote, work, line, self.sems, (1, slot), p.z_pair)
        across = functools.partial(remote, work, mid, self.sems, (2, slot), p.z_mid)
        outward = functools.partial(remote, done, done, self.sems, (3, slot), p.z_pair)
        back = functools.partial(remote, done, total.at[own], self.sems, (4, slot), p.y)
        fetch = functools.partial(pltpu.make_async_copy, part.at[own], work, self.local.at[0, slot])
        store = functools.partial(pltpu.make_async_copy, done, total.at[own], self.local.at[1, slot])

        if s == 0:
            beside().start()
            fetch().start()
        if s == 1:
            fetch().wait()
            beside().wait_recv()
            work[...] += land[...]

            @pl.when(p.end)
            def _():
                inward().start()

        if s in (2, 3):

            @pl.when(p.middle)
            def _():
                if s == 2:
                    inward().wait_recv()
                    work[...] += line[...]
                    across().start()
                if s == 3:
                    across().wait_recv()
                    done[...] = work[...] + mid[...]
                    outward().start()

        if s == 4:

            @pl.when(p.end)
            def _():
                outward().wait_recv()

            back().start()
            store().start()
        if s == 5:
            back().wait()
            beside().wait_send()
            store().wait()

            @pl.when(p.end)
            def _():
                inward().wait_send()

            @pl.when(p.middle)
            def _():
                across().wait_send()
                outward().wait_send()

    def tick(self, t):
        for s in reversed(range(STAGES)):
            if 0 <= t - s < len(self.chunks):
                self.stage(t - s, s)


class SmallSum:
    def __init__(self, peers, scratch):
        self.p = peers
        self.kept, self.got, self.sems = scratch

    @staticmethod
    def scratch():
        return [
            pltpu.VMEM((6, 8, 1024), jnp.float32),
            pltpu.VMEM((5, 8, 1024), jnp.float32),
            pltpu.SemaphoreType.DMA((2, 5)),
        ]

    def copy(self, s):
        p = self.p
        partner = (p.y, p.z_pair, p.z_far, p.core, p.x)[s]
        return remote(self.kept.at[s], self.got.at[s], self.sems, (s,), partner)

    def start(self, rows):
        self.kept[0] = rows
        self.copy(0).start()

    def step(self, s):
        self.copy(s).wait()
        self.kept[s + 1] = self.kept[s] + self.got[s]
        if s < 4:
            self.copy(s + 1).start()


class TensorSum:
    def __init__(self, peers, chunks, arrays, scratch):
        self.p, self.chunks = peers, chunks
        self.x, self.cot, self.vecs, self.output, self.grad_input = arrays
        self.land, self.work, self.mid, self.done, self.sems, self.local = scratch[:6]
        self.rows_x, self.rows_cot, self.rows_out, self.rows_grad, self.sem = scratch[6:]
        self.push = {}

    @staticmethod
    def scratch():
        f32, bf16 = jnp.float32, jnp.bfloat16
        return [
            pltpu.VMEM((2, TILE // 2, 1024), f32),
            pltpu.VMEM((3, TILE // 2, 1024), f32),
            pltpu.VMEM((4, TILE // 2, 1024), f32),
            pltpu.VMEM((2, TILE, 1024), f32),
            pltpu.SemaphoreType.DMA((2, 3, 4)),
            pltpu.SemaphoreType.DMA((3,)),
            pltpu.VMEM((TILE, 1024), bf16),
            pltpu.VMEM((TILE, 1024), bf16),
            pltpu.VMEM((TILE, 1024), bf16),
            pltpu.VMEM((TILE, 1024), f32),
            pltpu.SemaphoreType.DMA((4,)),
        ]

    def settle(self):
        for copy in self.push.values():
            copy.wait()
        self.push = {}

    def stage(self, c, s):
        p, half = self.p, TILE // 2
        part, row, backward = self.chunks[c]
        rows = pl.ds(row, TILE)
        own = pl.ds(pl.multiple_of(row + p.core_half * half, half), half)
        other = pl.ds(pl.multiple_of(row + (1 - p.core_half) * half, half), half)
        own_done = self.done.at[c % 2, pl.ds(pl.multiple_of(p.core_half * half, half), half)]
        land, work, mid = self.land.at[c % 2], self.work.at[c % 3], self.mid.at[c % 4]
        beside = functools.partial(remote, part.at[other], land, self.sems, (0, c % 2), p.core)
        across = functools.partial(remote, work, mid, self.sems, (1, c % 4), p.x)
        back = functools.partial(remote, own_done, own_done, self.sems, (2, c % 2), p.core)
        fetch = functools.partial(pltpu.make_async_copy, part.at[own], work, self.local.at[c % 3])
        get_x = functools.partial(
            pltpu.make_async_copy, self.x.at[rows], self.rows_x, self.sem.at[0]
        )
        get_cot = functools.partial(
            pltpu.make_async_copy, self.cot.at[rows], self.rows_cot, self.sem.at[1]
        )
        if s == 0:
            beside().start()
            fetch().start()
        if s == 1:
            fetch().wait()
            beside().wait()
            work[...] += land[...]
            across().start()
        if s == 2:
            get_x().start()
            if backward:
                get_cot().start()
            across().wait()
            own_done[...] = work[...] + mid[...]
            back().start()
        if s == 3:
            get_x().wait()
            if backward:
                get_cot().wait()
            back().wait()
            if backward in self.push:
                self.push.pop(backward).wait()
            total = self.done[c % 2]
            if backward:
                standard, inv_std = standardize(self.rows_x[...])
                scaled = total * self.vecs[0:1]
                inner = (
                    scaled
                    - jnp.mean(scaled, axis=1, keepdims=True)
                    - standard * jnp.mean(scaled * standard, axis=1, keepdims=True)
                )
                self.rows_grad[...] = self.rows_cot[...].astype(jnp.float32) + inv_std * inner
                copy = pltpu.make_async_copy(
                    self.rows_grad, self.grad_input.at[rows], self.sem.at[3]
                )
            else:
                biases = self.vecs[3:4] + self.vecs[4:5]
                result = self.rows_x[...].astype(jnp.float32) + total + biases
                self.rows_out[...] = result.astype(jnp.bfloat16)
                copy = pltpu.make_async_copy(self.rows_out, self.output.at[rows], self.sem.at[2])
            copy.start()
            self.push[backward] = copy

    def tick(self, t):
        for s, delay in reversed(list(enumerate(X_DELAYS))):
            if 0 <= t - delay < len(self.chunks):
                self.stage(t - delay, s)


def chunk_lists(parts, totals):
    ways = ([], [])
    for turn, (part, total) in enumerate(zip(parts, totals)):
        starts = np.arange(0, part.shape[0], CHUNK)
        if turn == 3:
            starts = starts.reshape(3, -1, PAIR // CHUNK).transpose(1, 0, 2).reshape(-1)
        for i, start in enumerate(starts.tolist()):
            ways[(turn if turn < 2 else i) % 2].append((part, total, start, part.shape[1]))
    return ways


def deliver_kernel(
    heads, output, grad_input, w_out, w_in, w_dense, w_qkv, small, *rest
):
    outs, held_whole, rest = rest[:12], rest[12:16], rest[16:]
    land, land_qkv, turned, turned_qkv, whole_sem, land_sem, turn_sem = rest
    to_output, to_grad, gain, shift, to_w_qkv, b_qkv, to_w_dense, b_dense, to_w_in, b_in = outs[:10]
    to_w_out, b_out = outs[10:]
    d, width = w_in.shape[1], heads * HD
    pending = []

    def begin(src, dst, sem):
        copy = pltpu.make_async_copy(src, dst, sem)
        copy.start()
        return copy

    blocks = []
    for b in range(w_in.shape[0] // TILE):
        rows = pl.ds(b * TILE, TILE)
        copy = begin(w_in.at[rows], land.at[rows], land_sem.at[len(blocks)])
        blocks.append(([copy], land, turned, to_w_in, b))
    for b in range(3 * width // TILE):
        copies = []
        for piece in range(b * TILE // HD, (b + 1) * TILE // HD):
            head, part = piece // 3, piece % 3
            src = w_qkv.at[pl.ds(part * width + head * HD, HD)]
            dst = land_qkv.at[pl.ds(piece * HD, HD)]
            copies.append(begin(src, dst, land_sem.at[w_in.shape[0] // TILE + piece]))
        blocks.append((copies, land_qkv, turned_qkv, to_w_qkv, b))
    wholes = []
    pairs = ((grad_input, to_grad), (output, to_output), (w_out, to_w_out), (w_dense, to_w_dense))
    for n, (src, dst) in enumerate(pairs):
        quarter = src.shape[0] // 4
        for i in range(4):
            rows = pl.ds(i * quarter, quarter)
            copy = begin(src.at[rows], held_whole[n].at[rows], whole_sem.at[0, n, i])
            wholes.append((copy, held_whole[n].at[rows], dst.at[rows], whole_sem.at[1, n, i]))

    def pass_on(count):
        for copy, held, dst, sem in wholes[:count]:
            copy.wait()
            pending.append(begin(held, dst, sem))
        del wholes[:count]

    for n, (copies, held, moved, target, b) in enumerate(blocks):
        for copy in copies:
            copy.wait()
        cols = pl.ds(b * TILE, TILE)
        moved[:, cols] = held[cols].T
        pending.append(begin(moved.at[:, cols], target.at[:, cols], turn_sem.at[n]))
        pass_on(3)
    pass_on(len(wholes))
    gain[...], shift[...], b_in[...] = small[8:9], small[9:10], small[3:4]
    b_dense[...] = small[2:3]
    b_out[...] = small[2:3]
    row = small[4:5, 0 : 3 * width]
    pieces = [
        row[:, part * width + head * HD : part * width + (head + 1) * HD]
        for head in range(heads)
        for part in range(3)
    ]
    b_qkv[...] = jnp.concatenate(pieces, axis=1)
    for copy in pending:
        copy.wait()


def deliver(output, grad_input, w_out, w_in, w_dense, w_qkv, small):
    f32 = jnp.float32
    (ff, d), width = w_in.shape, w_dense.shape[0]
    vm = pl.BlockSpec(memory_space=pltpu.VMEM)
    hbm = pl.BlockSpec(memory_space=pl.ANY)

    def shape(*dims):
        return jax.ShapeDtypeStruct(dims, f32)

    outs = pl.pallas_call(
        functools.partial(deliver_kernel, width // HD),
        out_shape=(
            jax.ShapeDtypeStruct(output.shape, output.dtype),
            shape(*grad_input.shape),
            shape(1, d),
            shape(1, d),
            shape(d, 3 * width),
            shape(1, 3 * width),
            shape(width, d),
            shape(1, d),
            shape(d, ff),
            shape(1, ff),
            shape(ff, d),
            shape(1, d),
        ),
        in_specs=[hbm] * 6 + [vm],
        out_specs=(hbm, hbm, vm, vm, hbm, vm, hbm, vm, hbm, vm, hbm, vm),
        scratch_shapes=[
            pltpu.VMEM(grad_input.shape, f32),
            pltpu.VMEM(output.shape, output.dtype),
            pltpu.VMEM(w_out.shape, f32),
            pltpu.VMEM(w_dense.shape, f32),
            pltpu.VMEM((ff, d), f32),
            pltpu.VMEM((3 * width, d), f32),
            pltpu.VMEM((d, ff), f32),
            pltpu.VMEM((d, 3 * width), f32),
            pltpu.SemaphoreType.DMA((2, 4, 4)),
            pltpu.SemaphoreType.DMA((ff // TILE + 3 * width // HD,)),
            pltpu.SemaphoreType.DMA((ff // TILE + 3 * width // TILE,)),
        ],
        compiler_params=pltpu.CompilerParams(vmem_limit_bytes=60 << 20),
        name="deliver",
    )(output, grad_input, w_out, w_in, w_dense, w_qkv, small)
    return tuple(o[0] if o.shape[0] == 1 else o for o in outs)


def rest_groups(dp_size):
    stride = z_stride(dp_size)
    places = np.arange(dp_size).reshape(-1, 4, stride // 2, 2)
    return places.transpose(1, 3, 0, 2).reshape(8, -1).tolist()


def on_device(
    dp_size,
    layer_input,
    positions,
    block_ids,
    ln_gain,
    ln_bias,
    w_qkv,
    b_qkv,
    w_dense,
    b_dense,
    w_in,
    b_in,
    w_out,
    b_out,
    cotangent,
):
    d = layer_input.shape[1]
    width = w_dense.shape[0]
    heads = width // HD
    frequency = rotary_base ** (-jnp.arange(0, ROT, 2).astype(jnp.float32) / ROT)
    phases = frequency[:, None] * positions.astype(jnp.float32)[None, :]
    trig = jnp.concatenate([jnp.cos(phases), jnp.sin(phases)], axis=0)
    bias = b_qkv.reshape(heads, 3, HD).transpose(1, 0, 2).reshape(3 * width)
    none = jnp.zeros((d,), jnp.float32)
    rows = [ln_gain, ln_bias, b_in, b_dense, b_out, jnp.pad(bias, (0, d - 3 * width)), none, none]
    output, grad_input, *sums = layer_call(
        dp_size,
        block_ids.astype(jnp.float32)[None, :],
        trig,
        jnp.stack(rows),
        w_dense,
        layer_input,
        cotangent,
        w_qkv,
        w_in,
        w_out,
    )
    if dp_size > 8:
        sums = lax.psum(sums, "dp", axis_index_groups=rest_groups(dp_size))
    return deliver(output, grad_input, *sums)


def solution(mesh):
    in_specs = (
        P("dp", None),
        P("dp"),
        P("dp"),
        P(),
        P(),
        P(None, "tensor"),
        P("tensor"),
        P("tensor", None),
        P(),
        P(None, "tensor"),
        P("tensor"),
        P("tensor", None),
        P(),
        P("dp", None),
    )
    out_specs = (
        P("dp", None),
        P("dp", None),
        P(),
        P(),
        P(None, "tensor"),
        P("tensor"),
        P("tensor", None),
        P(),
        P(None, "tensor"),
        P("tensor"),
        P("tensor", None),
        P(),
    )
    return jax.shard_map(
        functools.partial(on_device, mesh.shape["dp"]), mesh=mesh, in_specs=in_specs, out_specs=out_specs, check_vma=False
    )
```

```python
import functools

import jax
import jax.numpy as jnp
import numpy as np
from jax import lax
from jax.experimental import pallas as pl
from jax.experimental.pallas import tpu as pltpu
from jax.sharding import PartitionSpec as P

HD = 64
ROT = 16
TILE = 256

eps = 1e-05
rotary_base = 10000.0
NT = (((1,), (1,)), ((), ()))
TN = (((0,), (0,)), ((), ()))
NN = (((1,), (0,)), ((), ()))


def mm(a, b, dims=NN):
    return lax.dot_general(a, b, dims, preferred_element_type=jnp.float32)


def layer_kernel(
    heads,
    dp_size,
    ids_row,
    trig,
    vecs,
    w_dense,
    x_hbm,
    cot_hbm,
    w_qkv_hbm,
    w_in_hbm,
    w_out_hbm,
    output,
    grad_input,
    sum_w_out,
    sum_w_in,
    sum_w_dense,
    sum_w_qkv,
    small_sum,
    out_part,
    dnorm_part,
    gw_out,
    gw_in,
    gw_dense,
    gw_qkv,
    act_hbm,
    dh_hbm,
    q,
    k,
    v,
    q_t,
    k_t,
    v_t,
    do,
    do_t,
    scores,
    probs,
    normed,
    wide,
    stack_a,
    stack_b,
    dk,
    dv,
    dq_t,
    mixed,
    lse,
    delta,
    ids_col,
    w_in,
    w_out,
    w_cols,
    rows_sum,
    stage_h,
    stage_x,
    stage_out,
    stage_w,
    big_sem,
    h_sem,
    x_sem,
    out_sem,
    w_sem,
    spill_sem,
    *comm,
):
    tokens, d = x_hbm.shape
    tiles = tokens // TILE
    width = heads * HD
    ff = w_out.shape[0]
    f32, bf16 = jnp.float32, jnp.bfloat16
    parts = len(LineFirst.scratch())
    peers = Peers(dp_size)
    line, side = chunk_lists(
        (gw_out, gw_in, gw_dense, gw_qkv), (sum_w_out, sum_w_in, sum_w_dense, sum_w_qkv)
    )
    line_sum = LineFirst(peers, line, comm[:parts])
    side_sum = SideFirst(peers, side, comm[parts : 2 * parts])
    little = SmallSum(peers, comm[2 * parts : 2 * parts + 3])
    tensor_sum = TensorSum(
        peers,
        [(out_part, t * TILE, False) for t in range(tiles)]
        + [(dnorm_part, t * TILE, True) for t in reversed(range(tiles))],
        (x_hbm, cot_hbm, vecs, output, grad_input),
        comm[2 * parts + 3 :],
    )
    rounds = max(len(line), len(side)) + STAGES - 1
    state = {"d": 0, "x": 0, "made": 0, "push": None, "ready": 0, "due_d": 0.0, "due_x": 0.0}

    def settle():
        if state["push"] is not None:
            state["push"].wait()
            state["push"] = None

    def tick_x():
        n, last = state["x"], len(tensor_sum.chunks)
        if n < min(state["made"], last) or (state["made"] == last and n < last + X_DELAYS[-1]):
            settle()
            tensor_sum.tick(n)
            state["x"] += 1
            return True
        return False

    def tick_d():
        n = state["d"]
        if n < (state["ready"] if state["ready"] < len(line) else rounds):
            line_sum.tick(n)
            side_sum.tick(n)
            state["d"] += 1
            return True
        return False

    def worked(us):
        for way, pace, step in (("due_d", D_PACE, tick_d), ("due_x", X_PACE, tick_x)):
            state[way] = min(state[way] + us, 2 * pace)
            if state[way] >= pace and step():
                state[way] -= pace

    def begin(src, dst, sem):
        copy = pltpu.make_async_copy(src, dst, sem)
        copy.start()
        return copy

    def tile_rows(t):
        return pl.ds(t * TILE, TILE)

    lane_head = lax.broadcasted_iota(jnp.int32, (1, width), 1) >> 6
    row_head = lax.broadcasted_iota(jnp.int32, (width, 1), 0) >> 6

    def head_lanes(h):
        return (lane_head == h).astype(f32).astype(bf16)

    def head_rows(h):
        return (row_head == h).astype(f32).astype(bf16)

    peers.greet()
    qkv_copy = begin(w_qkv_hbm, w_in.at[:, pl.ds(0, 3 * width)], big_sem.at[0])
    x_copy = begin(x_hbm.at[tile_rows(0)], stage_x.at[0], x_sem.at[0])
    qkv_copy.wait()
    for part in range(3):
        pieces = [w_in[:, (3 * h + part) * HD : (3 * h + part + 1) * HD] for h in range(heads)]
        w_cols[:, part * width : (part + 1) * width] = jnp.concatenate(pieces, axis=1)

    gain, shift = vecs[0:1], vecs[1:2]
    for t in range(tiles):
        x_copy.wait()
        if t + 1 < tiles:
            slot = (t + 1) % 2
            next_copy = begin(x_hbm.at[tile_rows(t + 1)], stage_x.at[slot], x_sem.at[slot])
        if t == 0:
            w_in_copy = begin(w_in_hbm, w_in, big_sem.at[0])
        if t == 1:
            cot_copy = begin(cot_hbm, wide, big_sem.at[1])
        if t == 3:
            w_out_copy = begin(w_out_hbm, w_out, big_sem.at[2])
        standard, _ = standardize(stage_x[t % 2])
        normed[tile_rows(t)] = (standard * gain + shift).astype(bf16)
        x_copy = next_copy
        ids_tile = jnp.broadcast_to(ids_row[:, tile_rows(t)].astype(f32), (8, TILE))
        ids_col[tile_rows(t)] = ids_tile.T

    act_block, dh_block = mixed, do
    rows_sum[...] = jnp.zeros_like(rows_sum)
    cot_copy.wait()
    w_in_copy.wait()
    w_out_copy.wait()
    spills, puts = [], []

    def put_grad(value, part, row, slot):
        size = value.shape[0]
        stage_w[slot, 0:size] = value
        return begin(stage_w.at[slot, pl.ds(0, size)], part.at[pl.ds(row, size)], w_sem.at[slot])

    for c in range(ff // TILE):
        units = pl.ds(c * TILE, TILE)
        for copy in spills:
            copy.wait()
        for start in range(0, tokens, 2 * TILE):
            rows = pl.ds(start, 2 * TILE)
            hidden = mm(normed[rows], w_in[:, units]) + vecs[2:3, units]
            normal_cdf = 0.5 * (1.0 + lax.erf(hidden * 0.7071067811865476))
            act_block[rows] = (hidden * normal_cdf).astype(bf16)
            normal_pdf = jnp.exp(-0.5 * hidden * hidden) * 0.3989422804014327
            d_active = mm(wide[rows], w_out[units], NT)
            d_hidden = (d_active * (normal_cdf + hidden * normal_pdf)).astype(bf16)
            dh_block[rows] = d_hidden
            rows_sum[3:4, units] += jnp.sum(d_hidden.astype(f32), axis=0, keepdims=True)
        spills = [
            begin(act_block, act_hbm.at[:, units], spill_sem.at[0]),
            begin(dh_block, dh_hbm.at[:, units], spill_sem.at[1]),
        ]
        worked(3.6)
        puts = [
            put_grad(mm(act_block[...], wide[...], TN), gw_out, c * TILE, 0),
            put_grad(mm(dh_block[...], normed[...], TN), gw_in, c * TILE, 1),
        ]
        for copy in puts:
            copy.wait()
        state["ready"] += TILE // CHUNK
        worked(2.4)
    for copy in spills:
        copy.wait()

    half = ROT // 2
    still = jnp.ones((HD - ROT, TILE), f32)
    none = jnp.zeros((HD - ROT, TILE), f32)
    blank = jnp.zeros((half, TILE), f32)

    def lane_tables(cols):
        cosine, sine = trig[0:half, cols], trig[half : 2 * half, cols]
        cos_head = [cosine, cosine, still]
        low_head = [-sine, blank, none]
        high_head = [blank, sine, none]
        return tuple(jnp.concatenate(t + t, axis=0).T for t in (cos_head, low_head, high_head))

    def turn(value, tables, sign):
        cos_t, low_t, high_t = tables
        halves = []
        for part in range(value.shape[1] // 128):
            g = value[:, part * 128 : (part + 1) * 128]
            moved = pltpu.roll(g, 120, 1) * low_t + pltpu.roll(g, 8, 1) * high_t
            halves.append(g * cos_t + sign * moved)
        return jnp.concatenate(halves, axis=1)

    for t in range(tiles):
        rows = tile_rows(t)
        tables = lane_tables(rows)
        projected = mm(normed[rows], w_cols[...]) + vecs[5:6, 0 : 3 * width]
        query = turn(projected[:, 0:width], tables, 1.0).astype(bf16) * HD**-0.5
        key = turn(projected[:, width : 2 * width], tables, 1.0).astype(bf16)
        value = projected[:, 2 * width :].astype(bf16)
        d_out = mm(wide[rows], w_dense[...], NT).astype(bf16)
        q[rows], k[rows], v[rows], do[rows] = query, key, value, d_out
        q_t[:, rows], k_t[:, rows], v_t[:, rows], do_t[:, rows] = query.T, key.T, value.T, d_out.T
        rows_sum[2:3] += jnp.sum(wide[rows].astype(f32), axis=0, keepdims=True)
        worked(0.7)

    def send_out(value, part, rows):
        settle()
        stage_out[...] = value
        state["push"] = begin(stage_out, part.at[rows], out_sem)
        state["made"] += 1

    def span(i):
        return min(i + 2, tiles) * TILE

    for i in range(tiles):
        n, cols = span(i), tile_rows(i)
        fetch = begin(act_hbm.at[cols], stage_h, h_sem)

        def head_forward(h, _):
            rows = pl.ds(pl.multiple_of(h * HD, HD), HD)
            q_head = q_t[:, cols] * head_rows(h)
            top = None
            for start in range(0, n, TILE):
                keys = pl.ds(start, TILE)
                tile_scores = mm(k[keys], q_head)
                if start >= i * TILE:
                    allowed = ids_col[keys, 0:1] <= ids_row[:, cols].astype(f32)
                    tile_scores = jnp.where(allowed, tile_scores, -1e30)
                scores[keys] = tile_scores
                tile_top = jnp.max(tile_scores, axis=0, keepdims=True)
                top = tile_top if top is None else jnp.maximum(top, tile_top)
            total = jnp.zeros_like(top)
            for start in range(0, n, TILE):
                keys = pl.ds(start, TILE)
                weights = jnp.exp(scores[keys] - top)
                total += jnp.sum(weights, axis=0, keepdims=True)
                probs[keys, 0:TILE] = weights.astype(bf16)
            head_out = mm(v_t[rows, 0:n], probs[0:n, 0:TILE]) / total
            lse[pl.ds(h, 1), cols] = top + jnp.log(total)
            delta[pl.ds(h, 1), cols] = jnp.sum(
                head_out * do_t[rows, cols].astype(f32), axis=0, keepdims=True
            )
            dq_t[rows, cols] = head_out
            return 0

        lax.fori_loop(0, heads, head_forward, 0)
        mixed_tile = dq_t[:, cols].T.astype(bf16)
        mixed[cols] = mixed_tile
        fetch.wait()
        send_out(mm(mixed_tile, w_dense[...]) + mm(stage_h[...], w_out[...]), out_part, cols)
        worked(1.1 * n / TILE + 0.6)

    put_grad(mm(mixed[...], wide[...], TN), gw_dense, 0, 0).wait()
    state["ready"] += width // (2 * CHUNK)
    worked(0.8)

    def finish(pair, t, copies):
        rows = tile_rows(t)
        lanes = pl.ds(pair * PAIR, PAIR)
        tables = lane_tables(rows)
        dq_tile = turn(dq_t[lanes, rows].T * (HD**-0.5), tables, -1.0).astype(bf16)
        dk_tile = turn(dk[rows, lanes], tables, -1.0).astype(bf16)
        dv_tile = dv[rows, lanes].astype(bf16)
        for part, (held, piece) in enumerate(((q, dq_tile), (k, dk_tile), (v, dv_tile))):
            held[rows, lanes] = piece
            place = pl.ds(part * width + pair * PAIR, PAIR)
            rows_sum[4:5, place] += jnp.sum(piece.astype(f32), axis=0, keepdims=True)
        if pair < width // PAIR - 1:
            return
        for copy in copies:
            copy.wait()
        d_tile = mm(stage_h[...], w_in[...], NT)
        for part, held in enumerate((q, k, v)):
            d_tile += mm(held[rows], w_cols[:, part * width : (part + 1) * width], NT)
        send_out(d_tile, dnorm_part, rows)
        standard, _ = standardize(stage_x[0])
        rows_sum[0:1] += jnp.sum(d_tile * standard, axis=0, keepdims=True)
        rows_sum[1:2] += jnp.sum(d_tile, axis=0, keepdims=True)

    def fetches(t):
        rows = tile_rows(t)
        return (
            begin(dh_hbm.at[rows], stage_h, h_sem),
            begin(x_hbm.at[rows], stage_x.at[0], x_sem.at[0]),
        )

    lane_in_pair = lax.broadcasted_iota(jnp.int32, (1, PAIR), 1) >> 6
    row_in_pair = lax.broadcasted_iota(jnp.int32, (PAIR, 1), 0) >> 6
    for pair in range(width // PAIR):
        last = pair == width // PAIR - 1
        lanes = pl.ds(pair * PAIR, PAIR)
        for i in reversed(range(tiles)):
            n, cols = span(i), tile_rows(i)
            copies = fetches(i + 1) if last and i < tiles - 1 else None
            for j in range(2):
                own = (lane_in_pair == j).astype(f32).astype(bf16)
                stack_a[j * TILE : (j + 1) * TILE] = do[cols, lanes] * own
                stack_b[j * TILE : (j + 1) * TILE] = q[cols, lanes] * own

            def head_backward(j, _):
                h = 2 * pair + j
                rows = pl.ds(pl.multiple_of(h * HD, HD), HD)
                block = pl.ds(pl.multiple_of(j * TILE, TILE), TILE)
                d_block = pl.ds(pl.multiple_of((2 + j) * TILE, TILE), TILE)
                own = (row_in_pair == j).astype(f32).astype(bf16)
                q_head, do_head = q_t[lanes, cols] * own, do_t[lanes, cols] * own
                top, row_delta = lse[pl.ds(h, 1), cols], delta[pl.ds(h, 1), cols]
                for start in range(0, n, TILE):
                    keys = pl.ds(start, TILE)
                    tile_scores = mm(k[keys, lanes], q_head)
                    if start >= i * TILE:
                        allowed = ids_col[keys, 0:1] <= ids_row[:, cols].astype(f32)
                        tile_scores = jnp.where(allowed, tile_scores, -1e30)
                    weights = jnp.exp(tile_scores - top)
                    wide[keys, block] = weights.astype(bf16)
                    d_tile = weights * (mm(v[keys, lanes], do_head) - row_delta)
                    wide[keys, d_block] = d_tile.astype(bf16)
                dq_t[rows, cols] = mm(k_t[rows, 0:n], wide[0:n, d_block])
                return 0

            lax.fori_loop(0, 2, head_backward, 0)
            worked(0.5 * n / TILE)
            for grad, first, right in ((dv, 0, stack_a), (dk, 2 * TILE, stack_b)):
                for start in range(0, n, 2 * TILE):
                    keys = pl.ds(start, min(2 * TILE, n - start))
                    term = mm(wide[keys, pl.ds(first, 2 * TILE)], right[...])
                    grad[keys, lanes] = term if i == tiles - 1 else grad[keys, lanes] + term
            if i < tiles - 1:
                finish(pair, i + 1, copies)
            worked(0.15 * n / TILE + (1.4 if last else 0.5))
        finish(pair, 0, fetches(0) if last else None)
        if last:
            little.start(rows_sum[...])
        for part, held in enumerate((q, k, v)):
            term = mm(held[:, lanes], normed[...], TN)
            put_grad(term, gw_qkv, part * width + pair * PAIR, 0).wait()
        state["ready"] += 3 * PAIR // (2 * CHUNK)
        worked(2.5)

    for s in range(5):
        worked(D_PACE)
        little.step(s)
    small_sum[0:8] = little.kept[3]
    small_sum[8:16] = little.kept[5]
    while state["d"] < rounds:
        worked(D_PACE)
    while tick_x():
        pass
    tensor_sum.settle()


PAIR = 2 * HD
D_PACE = 8.4
X_PACE = 11.4
X_DELAYS = (0, 1, 3, 4)


def standardize(rows):
    centred = rows.astype(jnp.float32)
    centred = centred - jnp.mean(centred, axis=1, keepdims=True)
    inv_std = lax.rsqrt(jnp.mean(centred * centred, axis=1, keepdims=True) + eps)
    return centred * inv_std, inv_std


def layer_call(dp_size, ids_row, trig, vecs, w_dense, x, cot, w_qkv, w_in, w_out):
    tokens, d = x.shape
    width, ff = w_dense.shape[0], w_out.shape[0]
    heads = width // HD
    vm = pl.BlockSpec(memory_space=pltpu.VMEM)
    hbm = pl.BlockSpec(memory_space=pl.ANY)
    f32, bf16 = jnp.float32, jnp.bfloat16
    dma = pltpu.SemaphoreType.DMA
    scratch = [
        pltpu.VMEM((tokens, width), bf16),
        pltpu.VMEM((tokens, width), bf16),
        pltpu.VMEM((tokens, width), bf16),
        pltpu.VMEM((width, tokens), bf16),
        pltpu.VMEM((width, tokens), bf16),
        pltpu.VMEM((width, tokens), bf16),
        pltpu.VMEM((tokens, width), bf16),
        pltpu.VMEM((width, tokens), bf16),
        pltpu.VMEM((tokens, TILE), f32),
        pltpu.VMEM((tokens, TILE), bf16),
        pltpu.VMEM((tokens, d), bf16),
        pltpu.VMEM((tokens, d), bf16),
        pltpu.VMEM((2 * TILE, PAIR), bf16),
        pltpu.VMEM((2 * TILE, PAIR), bf16),
        pltpu.VMEM((tokens, width), f32),
        pltpu.VMEM((tokens, width), f32),
        pltpu.VMEM((width, tokens), f32),
        pltpu.VMEM((tokens, width), bf16),
        pltpu.VMEM((8, tokens), f32),
        pltpu.VMEM((8, tokens), f32),
        pltpu.VMEM((tokens, 8), f32),
        pltpu.VMEM((d, ff), bf16),
        pltpu.VMEM((ff, d), bf16),
        pltpu.VMEM((d, 3 * width), bf16),
        pltpu.VMEM((8, d), f32),
        pltpu.VMEM((TILE, ff), bf16),
        pltpu.VMEM((2, TILE, d), bf16),
        pltpu.VMEM((TILE, d), f32),
        pltpu.VMEM((2, TILE, d), f32),
        dma((3,)),
        dma,
        dma((2,)),
        dma,
        dma((2,)),
        dma((2,)),
    ]
    scratch += LineFirst.scratch() + SideFirst.scratch() + SmallSum.scratch() + TensorSum.scratch()

    def shape(*dims, dtype=f32):
        return jax.ShapeDtypeStruct(dims, dtype)

    outs = pl.pallas_call(
        functools.partial(layer_kernel, heads, dp_size),
        out_shape=(
            shape(tokens, d, dtype=bf16),
            shape(tokens, d),
            shape(ff, d),
            shape(ff, d),
            shape(width, d),
            shape(3 * width, d),
            shape(16, d),
            shape(tokens, d),
            shape(tokens, d),
            shape(ff, d),
            shape(ff, d),
            shape(width, d),
            shape(3 * width, d),
            shape(tokens, ff, dtype=bf16),
            shape(tokens, ff, dtype=bf16),
        ),
        in_specs=[vm] * 4 + [hbm] * 5,
        out_specs=(hbm,) * 6 + (vm,) + (hbm,) * 8,
        scratch_shapes=scratch,
        compiler_params=pltpu.CompilerParams(
            collective_id=0, has_side_effects=True, vmem_limit_bytes=63 << 20
        ),
        name="layer",
    )(ids_row, trig, vecs, w_dense, x, cot, w_qkv, w_in, w_out)
    return outs[:7]


SLOTS = 5
STAGES = 6
CHUNK = 64
MESH_ID = pl.DeviceIdType.MESH


def z_stride(group):
    return 2 if group == 8 else 4


class Peers:
    def __init__(self, dp_size):
        stride = z_stride(dp_size)
        d, t = lax.axis_index("dp"), lax.axis_index("tensor")
        z = lax.rem(lax.div(d, stride), 4)
        base = d - z * stride
        self.y_half = lax.rem(d, 2)
        self.z_half = lax.div(z, 2)
        self.middle = jnp.logical_or(z == 1, z == 2)
        self.end = jnp.logical_or(z == 0, z == 3)
        self.y = (d + 1 - 2 * self.y_half, t)
        self.z_pair = (base + stride * (z + 1 - 2 * lax.rem(z, 2)), t)
        self.z_mid = (base + stride * (3 - z), t)
        self.z_far = (base + stride * lax.rem(z + 2, 4), t)
        self.core_half = lax.rem(t, 2)
        self.core = (d, t + 1 - 2 * lax.rem(t, 2))
        self.x = (d, lax.rem(t + 2, 4))

    def greet(self):
        barrier = pltpu.get_barrier_semaphore()
        partners = (self.y, self.z_pair, self.z_mid, self.z_far, self.core, self.x)
        for partner in partners:
            pl.semaphore_signal(barrier, inc=1, device_id=partner, device_id_type=MESH_ID)
        pl.semaphore_wait(barrier, len(partners))


def remote(src, dst, sems, index, device):
    return pltpu.make_async_remote_copy(
        src_ref=src,
        dst_ref=dst,
        send_sem=sems.at[(0,) + index],
        recv_sem=sems.at[(1,) + index],
        device_id=device,
        device_id_type=MESH_ID,
    )


class LineFirst:
    def __init__(self, peers, chunks, scratch):
        self.p, self.chunks = peers, chunks
        self.land, self.work, self.mid, self.side, self.done, self.sems, self.local = scratch

    @staticmethod
    def scratch():
        f32 = jnp.float32
        return [
            pltpu.VMEM((SLOTS, CHUNK, 1024), f32),
            pltpu.VMEM((SLOTS, CHUNK, 1024), f32),
            pltpu.VMEM((SLOTS, CHUNK // 2, 1024), f32),
            pltpu.VMEM((SLOTS, CHUNK // 2, 1024), f32),
            pltpu.VMEM((SLOTS, CHUNK, 1024), f32),
            pltpu.SemaphoreType.DMA((2, 5, SLOTS)),
            pltpu.SemaphoreType.DMA((2, SLOTS)),
        ]

    def stage(self, c, s):
        p, slot = self.p, c % SLOTS
        part, total, row, cols = self.chunks[c]
        rows, lanes = pl.ds(row, CHUNK), pl.ds(0, cols)
        half = CHUNK // 2
        own = pl.ds(pl.multiple_of(p.z_half * half, half), half)
        other = pl.ds(pl.multiple_of((1 - p.z_half) * half, half), half)
        land, work = self.land.at[slot, :, lanes], self.work.at[slot, :, lanes]
        mid, side = self.mid.at[slot, :, lanes], self.side.at[slot, :, lanes]
        done = self.done.at[slot, :, lanes]
        inward = functools.partial(remote, part.at[rows], land, self.sems, (0, slot), p.z_pair)
        across = functools.partial(remote, work.at[other], mid, self.sems, (1, slot), p.z_mid)
        beside = functools.partial(remote, work.at[own], side, self.sems, (2, slot), p.y)
        back = functools.partial(remote, done.at[own], done.at[own], self.sems, (3, slot), p.z_mid)
        outward = functools.partial(remote, done, total.at[rows], self.sems, (4, slot), p.z_pair)
        fetch = functools.partial(pltpu.make_async_copy, part.at[rows], work, self.local.at[0, slot])
        store = functools.partial(pltpu.make_async_copy, done, total.at[rows], self.local.at[1, slot])

        if s == 0:

            @pl.when(p.end)
            def _():
                inward().start()

            @pl.when(p.middle)
            def _():
                fetch().start()

        if s == 5:

            @pl.when(p.end)
            def _():
                outward().wait_recv()
                inward().wait_send()

        if s > 0:

            @pl.when(p.middle)
            def _():
                if s == 1:
                    fetch().wait()
                    inward().wait_recv()
                    work[...] += land[...]
                    across().start()
                if s == 2:
                    across().wait_recv()
                    work[own] += mid[...]
                    beside().start()
                if s == 3:
                    beside().wait_recv()
                    done[own] = work[own] + side[...]
                    back().start()
                if s == 4:
                    back().wait_recv()
                    outward().start()
                    store().start()
                if s == 5:
                    for copy in (across, beside, back, outward):
                        copy().wait_send()
                    store().wait()

    def tick(self, t):
        for s in reversed(range(STAGES)):
            if 0 <= t - s < len(self.chunks):
                self.stage(t - s, s)


class SideFirst:
    def __init__(self, peers, chunks, scratch):
        self.p, self.chunks = peers, chunks
        self.land, self.work, self.line, self.mid, self.done, self.sems, self.local = scratch

    @staticmethod
    def scratch():
        return [pltpu.VMEM((SLOTS, CHUNK // 2, 1024), jnp.float32)] * 5 + [
            pltpu.SemaphoreType.DMA((2, 5, SLOTS)),
            pltpu.SemaphoreType.DMA((2, SLOTS)),
        ]

    def stage(self, c, s):
        p, slot = self.p, c % SLOTS
        part, total, row, cols = self.chunks[c]
        lanes, half = pl.ds(0, cols), CHUNK // 2
        own = pl.ds(pl.multiple_of(row + p.y_half * half, half), half)
        other = pl.ds(pl.multiple_of(row + (1 - p.y_half) * half, half), half)
        land, work = self.land.at[slot, :, lanes], self.work.at[slot, :, lanes]
        line, mid = self.line.at[slot, :, lanes], self.mid.at[slot, :, lanes]
        done = self.done.at[slot, :, lanes]
        beside = functools.partial(remote, part.at[other], land, self.sems, (0, slot), p.y)
        inward = functools.partial(remote, work, line, self.sems, (1, slot), p.z_pair)
        across = functools.partial(remote, work, mid, self.sems, (2, slot), p.z_mid)
        outward = functools.partial(remote, done, done, self.sems, (3, slot), p.z_pair)
        back = functools.partial(remote, done, total.at[own], self.sems, (4, slot), p.y)
        fetch = functools.partial(pltpu.make_async_copy, part.at[own], work, self.local.at[0, slot])
        store = functools.partial(pltpu.make_async_copy, done, total.at[own], self.local.at[1, slot])

        if s == 0:
            beside().start()
            fetch().start()
        if s == 1:
            fetch().wait()
            beside().wait_recv()
            work[...] += land[...]

            @pl.when(p.end)
            def _():
                inward().start()

        if s in (2, 3):

            @pl.when(p.middle)
            def _():
                if s == 2:
                    inward().wait_recv()
                    work[...] += line[...]
                    across().start()
                if s == 3:
                    across().wait_recv()
                    done[...] = work[...] + mid[...]
                    outward().start()

        if s == 4:

            @pl.when(p.end)
            def _():
                outward().wait_recv()

            back().start()
            store().start()
        if s == 5:
            back().wait()
            beside().wait_send()
            store().wait()

            @pl.when(p.end)
            def _():
                inward().wait_send()

            @pl.when(p.middle)
            def _():
                across().wait_send()
                outward().wait_send()

    def tick(self, t):
        for s in reversed(range(STAGES)):
            if 0 <= t - s < len(self.chunks):
                self.stage(t - s, s)


class SmallSum:
    def __init__(self, peers, scratch):
        self.p = peers
        self.kept, self.got, self.sems = scratch

    @staticmethod
    def scratch():
        return [
            pltpu.VMEM((6, 8, 1024), jnp.float32),
            pltpu.VMEM((5, 8, 1024), jnp.float32),
            pltpu.SemaphoreType.DMA((2, 5)),
        ]

    def copy(self, s):
        p = self.p
        partner = (p.y, p.z_pair, p.z_far, p.core, p.x)[s]
        return remote(self.kept.at[s], self.got.at[s], self.sems, (s,), partner)

    def start(self, rows):
        self.kept[0] = rows
        self.copy(0).start()

    def step(self, s):
        self.copy(s).wait()
        self.kept[s + 1] = self.kept[s] + self.got[s]
        if s < 4:
            self.copy(s + 1).start()


class TensorSum:
    def __init__(self, peers, chunks, arrays, scratch):
        self.p, self.chunks = peers, chunks
        self.x, self.cot, self.vecs, self.output, self.grad_input = arrays
        self.land, self.work, self.mid, self.done, self.sems, self.local = scratch[:6]
        self.rows_x, self.rows_cot, self.rows_out, self.rows_grad, self.sem = scratch[6:]
        self.push = {}

    @staticmethod
    def scratch():
        f32, bf16 = jnp.float32, jnp.bfloat16
        return [
            pltpu.VMEM((2, TILE // 2, 1024), f32),
            pltpu.VMEM((3, TILE // 2, 1024), f32),
            pltpu.VMEM((4, TILE // 2, 1024), f32),
            pltpu.VMEM((2, TILE, 1024), f32),
            pltpu.SemaphoreType.DMA((2, 3, 4)),
            pltpu.SemaphoreType.DMA((3,)),
            pltpu.VMEM((TILE, 1024), bf16),
            pltpu.VMEM((TILE, 1024), bf16),
            pltpu.VMEM((TILE, 1024), bf16),
            pltpu.VMEM((TILE, 1024), f32),
            pltpu.SemaphoreType.DMA((4,)),
        ]

    def settle(self):
        for copy in self.push.values():
            copy.wait()
        self.push = {}

    def stage(self, c, s):
        p, half = self.p, TILE // 2
        part, row, backward = self.chunks[c]
        rows = pl.ds(row, TILE)
        own = pl.ds(pl.multiple_of(row + p.core_half * half, half), half)
        other = pl.ds(pl.multiple_of(row + (1 - p.core_half) * half, half), half)
        own_done = self.done.at[c % 2, pl.ds(pl.multiple_of(p.core_half * half, half), half)]
        land, work, mid = self.land.at[c % 2], self.work.at[c % 3], self.mid.at[c % 4]
        beside = functools.partial(remote, part.at[other], land, self.sems, (0, c % 2), p.core)
        across = functools.partial(remote, work, mid, self.sems, (1, c % 4), p.x)
        back = functools.partial(remote, own_done, own_done, self.sems, (2, c % 2), p.core)
        fetch = functools.partial(pltpu.make_async_copy, part.at[own], work, self.local.at[c % 3])
        get_x = functools.partial(
            pltpu.make_async_copy, self.x.at[rows], self.rows_x, self.sem.at[0]
        )
        get_cot = functools.partial(
            pltpu.make_async_copy, self.cot.at[rows], self.rows_cot, self.sem.at[1]
        )
        if s == 0:
            beside().start()
            fetch().start()
        if s == 1:
            fetch().wait()
            beside().wait()
            work[...] += land[...]
            across().start()
        if s == 2:
            get_x().start()
            if backward:
                get_cot().start()
            across().wait()
            own_done[...] = work[...] + mid[...]
            back().start()
        if s == 3:
            get_x().wait()
            if backward:
                get_cot().wait()
            back().wait()
            if backward in self.push:
                self.push.pop(backward).wait()
            total = self.done[c % 2]
            if backward:
                standard, inv_std = standardize(self.rows_x[...])
                scaled = total * self.vecs[0:1]
                inner = (
                    scaled
                    - jnp.mean(scaled, axis=1, keepdims=True)
                    - standard * jnp.mean(scaled * standard, axis=1, keepdims=True)
                )
                self.rows_grad[...] = self.rows_cot[...].astype(jnp.float32) + inv_std * inner
                copy = pltpu.make_async_copy(
                    self.rows_grad, self.grad_input.at[rows], self.sem.at[3]
                )
            else:
                biases = self.vecs[3:4] + self.vecs[4:5]
                result = self.rows_x[...].astype(jnp.float32) + total + biases
                self.rows_out[...] = result.astype(jnp.bfloat16)
                copy = pltpu.make_async_copy(self.rows_out, self.output.at[rows], self.sem.at[2])
            copy.start()
            self.push[backward] = copy

    def tick(self, t):
        for s, delay in reversed(list(enumerate(X_DELAYS))):
            if 0 <= t - delay < len(self.chunks):
                self.stage(t - delay, s)


def chunk_lists(parts, totals):
    ways = ([], [])
    for turn, (part, total) in enumerate(zip(parts, totals)):
        starts = np.arange(0, part.shape[0], CHUNK)
        if turn == 3:
            starts = starts.reshape(3, -1, PAIR // CHUNK).transpose(1, 0, 2).reshape(-1)
        for i, start in enumerate(starts.tolist()):
            ways[(turn if turn < 2 else i) % 2].append((part, total, start, part.shape[1]))
    return ways


def deliver_kernel(
    heads, output, grad_input, w_out, w_in, w_dense, w_qkv, small, *rest
):
    outs, held_whole, rest = rest[:12], rest[12:16], rest[16:]
    land, land_qkv, turned, turned_qkv, whole_sem, land_sem, turn_sem = rest
    to_output, to_grad, gain, shift, to_w_qkv, b_qkv, to_w_dense, b_dense, to_w_in, b_in = outs[:10]
    to_w_out, b_out = outs[10:]
    d, width = w_in.shape[1], heads * HD
    pending = []

    def begin(src, dst, sem):
        copy = pltpu.make_async_copy(src, dst, sem)
        copy.start()
        return copy

    blocks = []
    for b in range(w_in.shape[0] // TILE):
        rows = pl.ds(b * TILE, TILE)
        copy = begin(w_in.at[rows], land.at[rows], land_sem.at[len(blocks)])
        blocks.append(([copy], land, turned, to_w_in, b))
    for b in range(3 * width // TILE):
        copies = []
        for piece in range(b * TILE // HD, (b + 1) * TILE // HD):
            head, part = piece // 3, piece % 3
            src = w_qkv.at[pl.ds(part * width + head * HD, HD)]
            dst = land_qkv.at[pl.ds(piece * HD, HD)]
            copies.append(begin(src, dst, land_sem.at[w_in.shape[0] // TILE + piece]))
        blocks.append((copies, land_qkv, turned_qkv, to_w_qkv, b))
    wholes = []
    pairs = ((grad_input, to_grad), (output, to_output), (w_out, to_w_out), (w_dense, to_w_dense))
    for n, (src, dst) in enumerate(pairs):
        quarter = src.shape[0] // 4
        for i in range(4):
            rows = pl.ds(i * quarter, quarter)
            copy = begin(src.at[rows], held_whole[n].at[rows], whole_sem.at[0, n, i])
            wholes.append((copy, held_whole[n].at[rows], dst.at[rows], whole_sem.at[1, n, i]))

    def pass_on(count):
        for copy, held, dst, sem in wholes[:count]:
            copy.wait()
            pending.append(begin(held, dst, sem))
        del wholes[:count]

    for n, (copies, held, moved, target, b) in enumerate(blocks):
        for copy in copies:
            copy.wait()
        cols = pl.ds(b * TILE, TILE)
        moved[:, cols] = held[cols].T
        pending.append(begin(moved.at[:, cols], target.at[:, cols], turn_sem.at[n]))
        pass_on(3)
    pass_on(len(wholes))
    gain[...], shift[...], b_in[...] = small[8:9], small[9:10], small[3:4]
    b_dense[...] = small[2:3]
    b_out[...] = small[2:3]
    row = small[4:5, 0 : 3 * width]
    pieces = [
        row[:, part * width + head * HD : part * width + (head + 1) * HD]
        for head in range(heads)
        for part in range(3)
    ]
    b_qkv[...] = jnp.concatenate(pieces, axis=1)
    for copy in pending:
        copy.wait()


def deliver(output, grad_input, w_out, w_in, w_dense, w_qkv, small):
    f32 = jnp.float32
    (ff, d), width = w_in.shape, w_dense.shape[0]
    vm = pl.BlockSpec(memory_space=pltpu.VMEM)
    hbm = pl.BlockSpec(memory_space=pl.ANY)

    def shape(*dims):
        return jax.ShapeDtypeStruct(dims, f32)

    outs = pl.pallas_call(
        functools.partial(deliver_kernel, width // HD),
        out_shape=(
            jax.ShapeDtypeStruct(output.shape, output.dtype),
            shape(*grad_input.shape),
            shape(1, d),
            shape(1, d),
            shape(d, 3 * width),
            shape(1, 3 * width),
            shape(width, d),
            shape(1, d),
            shape(d, ff),
            shape(1, ff),
            shape(ff, d),
            shape(1, d),
        ),
        in_specs=[hbm] * 6 + [vm],
        out_specs=(hbm, hbm, vm, vm, hbm, vm, hbm, vm, hbm, vm, hbm, vm),
        scratch_shapes=[
            pltpu.VMEM(grad_input.shape, f32),
            pltpu.VMEM(output.shape, output.dtype),
            pltpu.VMEM(w_out.shape, f32),
            pltpu.VMEM(w_dense.shape, f32),
            pltpu.VMEM((ff, d), f32),
            pltpu.VMEM((3 * width, d), f32),
            pltpu.VMEM((d, ff), f32),
            pltpu.VMEM((d, 3 * width), f32),
            pltpu.SemaphoreType.DMA((2, 4, 4)),
            pltpu.SemaphoreType.DMA((ff // TILE + 3 * width // HD,)),
            pltpu.SemaphoreType.DMA((ff // TILE + 3 * width // TILE,)),
        ],
        compiler_params=pltpu.CompilerParams(vmem_limit_bytes=60 << 20),
        name="deliver",
    )(output, grad_input, w_out, w_in, w_dense, w_qkv, small)
    return tuple(o[0] if o.shape[0] == 1 else o for o in outs)


def rest_groups(dp_size):
    stride = z_stride(dp_size)
    places = np.arange(dp_size).reshape(-1, 4, stride // 2, 2)
    return places.transpose(1, 3, 0, 2).reshape(8, -1).tolist()


def on_device(
    dp_size,
    layer_input,
    positions,
    block_ids,
    ln_gain,
    ln_bias,
    w_qkv,
    b_qkv,
    w_dense,
    b_dense,
    w_in,
    b_in,
    w_out,
    b_out,
    cotangent,
):
    d = layer_input.shape[1]
    width = w_dense.shape[0]
    heads = width // HD
    frequency = rotary_base ** (-jnp.arange(0, ROT, 2).astype(jnp.float32) / ROT)
    phases = frequency[:, None] * positions.astype(jnp.float32)[None, :]
    trig = jnp.concatenate([jnp.cos(phases), jnp.sin(phases)], axis=0)
    bias = b_qkv.reshape(heads, 3, HD).transpose(1, 0, 2).reshape(3 * width)
    none = jnp.zeros((d,), jnp.float32)
    rows = [ln_gain, ln_bias, b_in, b_dense, b_out, jnp.pad(bias, (0, d - 3 * width)), none, none]
    output, grad_input, *sums = layer_call(
        dp_size,
        block_ids[None, :],
        trig,
        jnp.stack(rows),
        w_dense,
        layer_input,
        cotangent,
        w_qkv,
        w_in,
        w_out,
    )
    if dp_size > 8:
        sums = lax.psum(sums, "dp", axis_index_groups=rest_groups(dp_size))
    return deliver(output, grad_input, *sums)


def solution(mesh):
    in_specs = (
        P("dp", None),
        P("dp"),
        P("dp"),
        P(),
        P(),
        P(None, "tensor"),
        P("tensor"),
        P("tensor", None),
        P(),
        P(None, "tensor"),
        P("tensor"),
        P("tensor", None),
        P(),
        P("dp", None),
    )
    out_specs = (
        P("dp", None),
        P("dp", None),
        P(),
        P(),
        P(None, "tensor"),
        P("tensor"),
        P("tensor", None),
        P(),
        P(None, "tensor"),
        P("tensor"),
        P("tensor", None),
        P(),
    )
    return jax.shard_map(
        functools.partial(on_device, mesh.shape["dp"]), mesh=mesh, in_specs=in_specs, out_specs=out_specs, check_vma=False
    )
```
